256 devices in a mesh: grp: 32 (over y, x, core), ctx: 8 (over z).
Axes of the slice: x: 4, y: 4, z: 8, core: 2. Of those that a mesh axis runs over, the one named last changes fastest.
Arguments:
- hidden: bfloat16 [65536, 3584], P(('grp', 'ctx')), may hold values from -6 to 6
- norm_gain: float32 [3584], replicated, may hold values from 0.1 to 1.9
- qkv_weight: bfloat16 [3584, 2304], P('grp'), may hold values from -4.008919 to 4.008919
- qkv_bias: float32 [2304], replicated, may hold values from -3 to 3
- repo_lengths: int32 [32, 6], P('grp'), may hold values from 1 to 1024, 2048 in all within a row
Outputs:
- context: bfloat16 [65536, 1792], P(('grp', 'ctx'))
The draws below stay inside these ranges and needn't reach their ends.
All inputs are finite; a program needn't handle non-finite values.
Results may differ from the reference program's by a relative error of at most 0.0059.
The reference program's roundings to bfloat16 on the way (of `normed`, `projected` and `rounded_weights`) count: a program that leaves them out, or rounds other values in their place, can miss the bound.
Values may be sent and summed in bfloat16 or wider, within the bound.
No kernel may reach another device: no remote copies, remote signals or barrier semaphores. Data moves between devices by JAX's collectives and lax.ppermute only.
A program may use at most 128 MiB of HBM per device.

```python
import math
import jax
import jax.numpy as jnp
import numpy as np
from jax import lax

D = 3584
HEAD_DIM = 128
HEADS = 14
KV_HEADS = 2
REPOS = 6
TOK_DEV = 256
LENGTH = 2048
SLICES = 32
QKV = 2304


def draw_qkv_weight(key, part):
    base = jnp.clip(jax.random.normal(key, (D, QKV), jnp.float32), -4.0, 4.0) * D ** (-0.5)
    return base.astype(jnp.bfloat16)


def level_of(own_key, extent, split, smallest, top_value):
    def one(dim, blocks):
        heights = jax.random.uniform(jax.random.fold_in(jax.random.fold_in(own_key, 6), dim), (blocks,), jnp.float32, smallest / len(split), top_value / len(split))
        return jnp.repeat(jnp.exp(heights), extent[dim] // blocks).reshape((-1,) + (1,) * (len(extent) - dim - 1))

    gain = one(*split[0])
    for cut in split[1:]:
        gain = gain * one(*cut)
    return gain


def length_profile(number_of, total, limit, lean):
    loads = [(1 << 20) // math.isqrt(standing ** lean) + 1 for standing in range(2, number_of + 1)]
    rest, holding = total - limit - (number_of - 1), [1] * (number_of - 1)
    while rest > 0:
        movable = [i for i in range(number_of - 1) if holding[i] < limit]
        whole, remaining = sum([loads[i] for i in movable]), rest
        for i in movable:
            more = min(limit - holding[i], max(1, remaining * loads[i] // whole), rest)
            holding[i] = holding[i] + more
            rest = rest - more
    return np.array([limit] + holding)


def ragged_sizes(stream_key, count, total, limit, lean):
    if count == 2:
        one = jax.random.randint(stream_key, (), max(1, total - limit), min(limit, total - 1) + 1)
        return jnp.stack([one, total - one])
    tallies = jnp.asarray(length_profile(count, total, limit, lean), jnp.int32)
    couples = (count - 1) // 2
    donor, taker = tallies[1:1 + 2 * couples:2], tallies[2:2 + 2 * couples:2]
    room = jnp.minimum(donor - 1, limit - taker)
    passed = jax.random.randint(jax.random.fold_in(stream_key, 1), (couples,), 0, 1 << 20) % (room + 1)
    tallies = tallies.at[1:1 + 2 * couples:2].set(donor - passed).at[2:2 + 2 * couples:2].set(taker + passed)
    return tallies[jax.random.permutation(jax.random.fold_in(stream_key, 2), count)]


def scatter_about(key, shape, spread, bound, cuts=(), held_as=jnp.bfloat16):
    level = level_of(key, shape, cuts, -0.22, 0.18) if cuts else 1.0
    values = jax.random.normal(key, shape, jnp.float32) * spread * level
    return jnp.minimum(jnp.maximum(values, -bound), bound).astype(held_as)


def setup_inputs(seed: int = 0) -> dict:
    seeds = jax.random.split(jax.random.key(seed), 6)
    return {
        "hidden": scatter_about(seeds[0], (SLICES * LENGTH, D), 1.0, 6.0, ((0, 256),)),
        "norm_gain": jnp.clip(1.0 + 0.18 * jax.random.normal(seeds[1], (D,), jnp.float32), 0.1, 1.9),
        "qkv_weight": draw_qkv_weight(jax.random.fold_in(seeds[5], 71), 0),
        "qkv_bias": scatter_about(seeds[3], (QKV,), 0.5, 3.0, (), jnp.float32),
        "repo_lengths": jax.vmap(lambda own: ragged_sizes(own, REPOS, LENGTH, LENGTH // 2, 2))(jax.random.split(seeds[4], SLICES)).reshape((SLICES, REPOS)).astype(jnp.int32),
    }


rope_base = 1000000.0
norm_eps = 1e-06

def rope_tables(position):
    inv_freq = rope_base ** (-jnp.arange(0, HEAD_DIM, 2, dtype=jnp.float32) / HEAD_DIM)
    angle = position.astype(jnp.float32)[:, None] * inv_freq[None, :]
    angle = jnp.concatenate([angle, angle], axis=-1)
    return (jnp.cos(angle), jnp.sin(angle))

def rotate(values, cosine, sine_part):
    half = HEAD_DIM // 2
    first = values[..., :half]
    second = values[..., half:]
    turned = jnp.concatenate([-second, first], axis=-1)
    return values * cosine[:, None, :] + turned * sine_part[:, None, :]

def repo_start_of(tok_index, lengths):
    repo_ends = jnp.cumsum(lengths)
    return lax.optimization_barrier(jnp.sum(jnp.where(tok_index[:, None] >= repo_ends[None, :], lengths[None, :], 0), axis=1)).astype(jnp.int32)

def reference(hidden, norm_gain, qkv_weight, qkv_bias, repo_lengths):
    return slices_run(hidden, repo_lengths, norm_gain, qkv_weight, qkv_bias)

def slices_run(hidden, repo_lengths, norm_gain, qkv_weight, qkv_bias):

    def per_slice(operands):
        return slice_work(operands[0], operands[1], norm_gain, qkv_weight, qkv_bias)
    outputs = lax.map(per_slice, (hidden.reshape(SLICES, LENGTH, D), repo_lengths))
    return outputs.reshape(SLICES * LENGTH, HEADS * HEAD_DIM)

def slice_work(hidden_rows, lengths, norm_gain, qkv_weight, qkv_bias):
    hidden_f32 = hidden_rows.astype(jnp.float32)
    normed = (hidden_f32 * lax.rsqrt(lax.optimization_barrier(jnp.mean(hidden_f32 * hidden_f32, axis=1, keepdims=True)) + norm_eps) * norm_gain[None, :]).astype(jnp.bfloat16)
    projected = (jnp.dot(normed, qkv_weight, preferred_element_type=jnp.float32) + qkv_bias[None, :]).astype(jnp.bfloat16)
    tok_index = jnp.arange(LENGTH, dtype=jnp.int32)
    repo_start = repo_start_of(tok_index, lengths)
    cosine, sine_part = rope_tables(tok_index - repo_start)
    q_cols = HEADS * HEAD_DIM
    k_cols = KV_HEADS * HEAD_DIM
    query_f32 = projected[:, :q_cols].astype(jnp.float32).reshape(LENGTH, HEADS, HEAD_DIM)
    key_f32 = projected[:, q_cols:q_cols + k_cols].astype(jnp.float32).reshape(LENGTH, KV_HEADS, HEAD_DIM)
    queries = rotate(query_f32, cosine, sine_part).astype(jnp.bfloat16).reshape(LENGTH, KV_HEADS, HEADS // KV_HEADS, HEAD_DIM)
    keys = rotate(key_f32, cosine, sine_part).astype(jnp.bfloat16)
    values = projected[:, q_cols + k_cols:].reshape(LENGTH, KV_HEADS, HEAD_DIM)
    blocks = LENGTH // TOK_DEV
    key_index = jnp.arange(LENGTH, dtype=jnp.int32)

    def one_block(block_ops):
        query_block, tok_block, start_block = block_ops
        scores = jnp.einsum('rgho,kgo->ghrk', query_block.astype(jnp.float32), keys.astype(jnp.float32)) * HEAD_DIM ** (-0.5)
        allowed = (key_index[None, :] <= tok_block[:, None]) & (key_index[None, :] >= start_block[:, None])
        scores = jnp.where(allowed, scores, -1e+30)
        row_max = lax.optimization_barrier(jnp.max(scores, axis=-1))
        weights = jnp.where(allowed, jnp.exp(scores - row_max[..., None]), 0.0)
        row_total = lax.optimization_barrier(jnp.sum(weights, axis=-1))
        rounded_weights = weights.astype(jnp.bfloat16)
        weighted = jnp.einsum('ghrk,kgo->ghro', rounded_weights.astype(jnp.float32), values.astype(jnp.float32), precision=lax.Precision.HIGHEST)
        result = weighted / row_total[..., None]
        return jnp.transpose(result, (2, 0, 1, 3)).reshape(TOK_DEV, HEADS * HEAD_DIM).astype(jnp.bfloat16)
    outputs = lax.map(one_block, (queries.reshape(blocks, TOK_DEV, KV_HEADS, HEADS // KV_HEADS, HEAD_DIM), tok_index.reshape(blocks, TOK_DEV), repo_start.reshape(blocks, TOK_DEV)))
    return outputs.reshape(LENGTH, HEADS * HEAD_DIM)
```

```python
import functools
import math

import jax
import jax.numpy as jnp
from jax import lax
from jax.experimental import pallas as pl
from jax.experimental.pallas import tpu as pltpu
from jax.sharding import Mesh
from jax.sharding import PartitionSpec as P

D = 3584
HEAD_DIM = 128
HEADS = 14
KV_HEADS = 2
GROUP = HEADS // KV_HEADS
LENGTH = 2048
TOK = 256
HALF = 128
ROWS = 512
WROWS = 112
QC = GROUP * HEAD_DIM
WINDOW = 1152
rope_base = 1000000.0
norm_eps = 1e-06
SCALE2 = HEAD_DIM ** (-0.5) * math.log2(math.e)
MASKED = -1e30
SIZES = {"x": 4, "y": 4, "core": 2, "ctx": 8}
ORDER = (0, -1, 1, 2)

ANY = pl.BlockSpec(memory_space=pl.ANY)
VM = pl.BlockSpec(memory_space=pltpu.VMEM)
SM = pl.BlockSpec(memory_space=pltpu.SMEM)


def params():
    return pltpu.CompilerParams(vmem_limit_bytes=48 << 20)


def ring(value, axis, step):
    n = SIZES[axis]
    return lax.ppermute(value, axis, [(i, (i + step) % n) for i in range(n)])


def gather_ring(own, first, second):
    row = jnp.concatenate(
        [own, ring(own, first, 1), ring(own, first, -1), ring(own, first, 2)], 0
    )
    below = ring(row, second, 1)
    above = ring(row, second, -1)
    half = row.shape[0] // 2
    far_top = ring(below[:half], second, 1)
    far_bottom = ring(above[half:], second, -1)
    return jnp.concatenate([row, below, above, far_top, far_bottom], 0)


def norm_kernel(before_ref, own_ref, after_ref, gain_ref, out_ref):
    gain = gain_ref[...]

    def rows(src, at, dst, count):
        value = src[pl.ds(at, count), :].astype(jnp.float32)
        mean = jnp.mean(value * value, axis=1, keepdims=True)
        out_ref[pl.ds(dst, count), :] = (value * lax.rsqrt(mean + norm_eps) * gain).astype(
            jnp.bfloat16
        )

    def run(src, dst, total):
        @pl.loop(0, total // 16)
        def _(i):
            at = pl.multiple_of(i * 16, 16)
            rows(src, at, pl.multiple_of(dst + i * 16, 16), 16)

    run(before_ref, 0, HALF)
    run(own_ref, HALF, TOK)
    run(after_ref, HALF + TOK, HALF)


def norm(before, own, after, gain):
    return pl.pallas_call(
        norm_kernel,
        out_shape=jax.ShapeDtypeStruct((ROWS, D), jnp.bfloat16),
        in_specs=[VM] * 4,
        out_specs=VM,
        compiler_params=params(),
        cost_estimate=pl.CostEstimate(
            flops=8 * ROWS * D, bytes_accessed=4 * ROWS * D, transcendentals=ROWS
        ),
        name="norm",
    )(before, own, after, gain.reshape(1, D))


def rotate(value, cosine, sine):
    return value * cosine + pltpu.roll(value, HEAD_DIM // 2, 1) * sine


def kv_kernel(at_ref, x_ref, k_ref, k_far_ref, v_ref, v_far_ref, bias_ref, cos_ref, sin_ref, out_ref, w_ref, sem):
    copies = []
    for piece, (src, lane) in enumerate(((k_ref, 0), (k_far_ref, 0), (v_ref, 128), (v_far_ref, 128))):
        for block in range(16):
            at = pl.multiple_of(at_ref[piece * 16 + block], 16)
            copy = pltpu.make_async_copy(
                src.at[pl.ds(block * WROWS, WROWS), :],
                w_ref.at[pl.ds(at, WROWS), pl.ds(lane, 128)],
                sem.at[piece * 16 + block],
            )
            copy.start()
            copies.append(copy)
    for copy in copies:
        copy.wait()

    @pl.loop(0, ROWS // 256)
    def _(i):
        rows = pl.ds(pl.multiple_of(i * 256, 256), 256)
        value = jnp.dot(x_ref[rows, :], w_ref[...], preferred_element_type=jnp.float32)
        value = (value + bias_ref[...]).astype(jnp.bfloat16)
        keys = rotate(value[:, :128].astype(jnp.float32), cos_ref[rows, :], sin_ref[rows, :])
        out_ref[rows, 0:128] = keys.astype(jnp.bfloat16)
        out_ref[rows, 128:256] = value[:, 128:]


def kv_project(at, x, pieces, bias, cosine, sine):
    return pl.pallas_call(
        kv_kernel,
        out_shape=jax.ShapeDtypeStruct((ROWS, 256), jnp.bfloat16),
        in_specs=[SM, VM, ANY, ANY, ANY, ANY, VM, VM, VM],
        out_specs=VM,
        scratch_shapes=[pltpu.VMEM((D, 256), jnp.bfloat16), pltpu.SemaphoreType.DMA((64,))],
        compiler_params=params(),
        cost_estimate=pl.CostEstimate(
            flops=2 * ROWS * D * 256, bytes_accessed=2 * (ROWS * D + D * 256), transcendentals=0
        ),
        name="kv_project",
    )(at, x, *pieces, bias, cosine, sine)


Q_CHUNKS = ((0, 256), (256, 256), (512, 256), (768, 128))


def q_kernel(x_ref, w_hbm, bias_ref, cos_ref, sin_ref, out_ref, w_ref, sem):
    copies = []
    for n, (at, wide) in enumerate(Q_CHUNKS):
        copy = pltpu.make_async_copy(
            w_hbm.at[:, pl.ds(at, wide)], w_ref.at[:, pl.ds(at, wide)], sem.at[n]
        )
        copy.start()
        copies.append(copy)
    for (at, wide), copy in zip(Q_CHUNKS, copies):
        copy.wait()

        @pl.loop(0, ROWS // 256)
        def _(i, at=at, wide=wide):
            rows = pl.ds(pl.multiple_of(i * 256, 256), 256)
            value = jnp.dot(
                x_ref[rows, :], w_ref[:, at : at + wide], preferred_element_type=jnp.float32
            )
            value = (value + bias_ref[:, at : at + wide]).astype(jnp.bfloat16).astype(jnp.float32)
            for lane in range(0, wide, 128):
                head = rotate(value[:, lane : lane + 128], cos_ref[rows, :], sin_ref[rows, :])
                out_ref[rows, at + lane : at + lane + 128] = head.astype(jnp.bfloat16)


def q_project(x, weight, bias, cosine, sine):
    return pl.pallas_call(
        q_kernel,
        out_shape=jax.ShapeDtypeStruct((ROWS, QC), jnp.bfloat16),
        in_specs=[VM, ANY, VM, VM, VM],
        out_specs=VM,
        scratch_shapes=[pltpu.VMEM((D, QC), jnp.bfloat16), pltpu.SemaphoreType.DMA((4,))],
        compiler_params=params(),
        cost_estimate=pl.CostEstimate(
            flops=2 * ROWS * D * QC, bytes_accessed=2 * (ROWS * D + D * QC), transcendentals=0
        ),
        name="q_project",
    )(x, weight, bias, cosine, sine)


def attention_kernel(tiles, base_ref, q_ref, kv4_ref, kv2_ref, kv0_ref, pos_ref, start_ref, *rest):
    outs = rest[: len(tiles)]
    kv_ref, score_ref, weight_ref, total_ref = rest[len(tiles) :]
    kv_ref[0:512, :] = kv4_ref[...]
    kv_ref[512:1024, :] = kv2_ref[...]
    kv_ref[1024:1536, :] = kv0_ref[...]
    for tile, out_ref in zip(tiles, outs):
        rows = slice(HALF * tile, HALF * (tile + 1))
        window = slice(HALF * tile, HALF * tile + WINDOW)
        q = jnp.concatenate(
            [q_ref[rows, h * HEAD_DIM : (h + 1) * HEAD_DIM] for h in range(GROUP)], 0
        )
        score_ref[...] = lax.dot_general(
            q,
            kv_ref[window, 0:128],
            (((1,), (1,)), ((), ())),
            preferred_element_type=jnp.float32,
        )
        key = lax.broadcasted_iota(jnp.int32, (HALF, WINDOW), 1) + (base_ref[0] + HALF * tile)
        key = jnp.where(key >= LENGTH, key - LENGTH, key)
        allowed = (key <= pos_ref[rows, :]) & (key >= start_ref[rows, :])
        mask = jnp.where(allowed, 0.0, MASKED)
        for h in range(GROUP):
            part = slice(h * HALF, (h + 1) * HALF)
            score = score_ref[part, :] * SCALE2 + mask
            top = jnp.max(score, axis=1, keepdims=True)
            weight = jnp.exp2(score - top)
            total_ref[part, :] = jnp.broadcast_to(
                jnp.sum(weight, axis=1, keepdims=True), (HALF, HEAD_DIM)
            )
            weight_ref[part, :] = weight.astype(jnp.bfloat16)
        mixed = jnp.dot(
            weight_ref[...], kv_ref[window, 128:256], preferred_element_type=jnp.float32
        )
        mixed = (mixed / total_ref[...]).astype(jnp.bfloat16)
        for h in range(GROUP):
            out_ref[:, h * HEAD_DIM : (h + 1) * HEAD_DIM] = mixed[h * HALF : (h + 1) * HALF]


def attention(tiles, base, q, kv4, kv2, kv0, pos, start):
    n = len(tiles)
    stack = GROUP * HALF
    return pl.pallas_call(
        functools.partial(attention_kernel, tiles),
        out_shape=[jax.ShapeDtypeStruct((HALF, QC), jnp.bfloat16)] * n,
        in_specs=[SM] + [VM] * 6,
        out_specs=[VM] * n,
        scratch_shapes=[
            pltpu.VMEM((1536, 256), jnp.bfloat16),
            pltpu.VMEM((stack, WINDOW), jnp.float32),
            pltpu.VMEM((stack, WINDOW), jnp.bfloat16),
            pltpu.VMEM((stack, HEAD_DIM), jnp.float32),
        ],
        compiler_params=params(),
        cost_estimate=pl.CostEstimate(
            flops=4 * n * stack * WINDOW * HEAD_DIM,
            bytes_accessed=4 << 20,
            transcendentals=n * stack * WINDOW,
        ),
        name="attention",
    )(base, q, kv4, kv2, kv0, pos, start)


def body(hidden, norm_gain, qkv_weight, qkv_bias, repo_lengths):
    z = lax.axis_index("ctx")
    odd = z % 2
    y, x, core = lax.axis_index("y"), lax.axis_index("x"), lax.axis_index("core")

    k_at, v_at = 1792 + odd * 128, 2048 + odd * 128
    k_own = lax.dynamic_slice(qkv_weight, (0, k_at), (WROWS, 128))
    v_own = lax.dynamic_slice(qkv_weight, (0, v_at), (WROWS, 128))
    q_own = lax.dynamic_slice(qkv_weight, (0, odd * QC), (WROWS, QC))
    q_bias = lax.dynamic_slice(qkv_bias, (odd * QC,), (QC,)).reshape(1, QC)
    kv_bias = jnp.concatenate(
        [lax.dynamic_slice(qkv_bias, (k_at,), (128,)), lax.dynamic_slice(qkv_bias, (v_at,), (128,))]
    ).reshape(1, 256)

    q_weight = lax.all_gather(q_own, ("y", "x", "core"), axis=0, tiled=True)
    k_weight = gather_ring(k_own, "x", "y")
    v_weight = gather_ring(v_own, "y", "x")
    before = ring(hidden[TOK - HALF :], "ctx", 1)
    after = ring(hidden[:HALF], "ctx", -1)
    k_far = ring(k_weight, "core", 1)
    v_far = ring(v_weight, "core", 1)

    outer = jnp.repeat(jnp.array(ORDER, jnp.int32), 4)
    inner = jnp.tile(jnp.array(ORDER, jnp.int32), 4)
    k_rows = (((y + outer) % 4) * 4 + (x + inner) % 4) * 2 * WROWS
    v_rows = (((y + inner) % 4) * 4 + (x + outer) % 4) * 2 * WROWS
    here, there = core * WROWS, (1 - core) * WROWS
    at = jnp.concatenate([k_rows + here, k_rows + there, v_rows + here, v_rows + there])

    lengths = repo_lengths[0]
    pos = (z * TOK - HALF + LENGTH + jnp.arange(ROWS, dtype=jnp.int32)) % LENGTH
    start = jnp.zeros((ROWS,), jnp.int32)
    end = jnp.int32(0)
    for r in range(repo_lengths.shape[1]):
        end = end + lengths[r]
        start = start + jnp.where(pos >= end, lengths[r], 0)
    inv_freq = rope_base ** (-jnp.arange(0, HEAD_DIM, 2, dtype=jnp.float32) / HEAD_DIM)
    angle = (pos - start).astype(jnp.float32)[:, None] * inv_freq[None, :]
    cosine, sine = jnp.cos(angle), jnp.sin(angle)
    cosine = jnp.concatenate([cosine, cosine], 1)
    sine = jnp.concatenate([-sine, sine], 1)

    normed = norm(before, hidden, after, norm_gain)
    kv0 = kv_project(at, normed, (k_weight, k_far, v_weight, v_far), kv_bias, cosine, sine)
    kv2 = ring(kv0, "ctx", 2)
    kv4 = ring(kv2, "ctx", 2)
    q = q_project(normed, q_weight, q_bias, cosine, sine)

    base = ((z * TOK - HALF - 1024 + LENGTH) % LENGTH).reshape(1)
    args = (base, q, kv4, kv2, kv0, pos.reshape(ROWS, 1), start.reshape(ROWS, 1))
    back, ahead = attention((0, 3), *args)
    low = ring(ahead, "ctx", 1)
    high = ring(back, "ctx", -1)
    own = jnp.concatenate(attention((1, 2), *args), 0)
    other = jnp.concatenate([low, high], 0)
    return jnp.where(
        odd == 0, jnp.concatenate([own, other], 1), jnp.concatenate([other, own], 1)
    )


def solution(mesh):
    fine = Mesh(mesh.devices.reshape(4, 4, 2, 8), ("y", "x", "core", "ctx"))
    grp = ("y", "x", "core")
    tokens = P(("y", "x", "core", "ctx"), None)
    in_specs = (tokens, P(), P(grp, None), P(), P(grp, None))
    return jax.shard_map(body, mesh=fine, in_specs=in_specs, out_specs=tokens, check_vma=False)
```

```python
import functools
import math

import jax
import jax.numpy as jnp
from jax import lax
from jax.experimental import pallas as pl
from jax.experimental.pallas import tpu as pltpu
from jax.sharding import Mesh
from jax.sharding import PartitionSpec as P

D = 3584
HEAD_DIM = 128
HEADS = 14
KV_HEADS = 2
GROUP = HEADS // KV_HEADS
LENGTH = 2048
TOK = 256
HALF = 128
ROWS = 512
WROWS = 112
REPOS = 6
QC = GROUP * HEAD_DIM
rope_base = 1000000.0
norm_eps = 1e-06
SCALE2 = HEAD_DIM ** (-0.5) * math.log2(math.e)
MASKED = -1e30
SIZES = {"x": 4, "y": 4, "core": 2, "ctx": 8}
ORDER = (0, -1, 1, 2)

VM = pl.BlockSpec(memory_space=pltpu.VMEM)
SM = pl.BlockSpec(memory_space=pltpu.SMEM)


def params(mebibytes):
    return pltpu.CompilerParams(vmem_limit_bytes=mebibytes << 20)


def ring(value, axis, step):
    n = SIZES[axis]
    return lax.ppermute(value, axis, [(i, (i + step) % n) for i in range(n)])


def hop(value, phase, step):
    pairs = []
    for y in range(4):
        for x in range(4):
            for core in range(2):
                to_y, to_x = (y, (x + step) % 4) if core == phase else ((y + step) % 4, x)
                pairs.append(((y * 4 + x) * 2 + core, (to_y * 4 + to_x) * 2 + core))
    return lax.ppermute(value, ("y", "x", "core"), pairs)


def first_phase(own):
    return jnp.concatenate([own, hop(own, 0, 1), hop(own, 0, -1), hop(own, 0, 2)], 0)


def place_weights(info_ref, pieces, chunks, w_refs):
    y, x = info_ref[0], info_ref[1]
    for side in range(2):
        core = info_ref[2] if side == 0 else 1 - info_ref[2]
        block = 0
        for piece in pieces[side]:
            for i in range(piece.shape[0] // WROWS):
                outer, inner = ORDER[block // 4], ORDER[block % 4]
                dy = jnp.where(core == 0, outer, inner)
                dx = jnp.where(core == 0, inner, outer)
                chip = ((y + dy + 4) % 4) * 4 + (x + dx + 4) % 4
                at = pl.multiple_of((chip * 2 + core) * WROWS, 16)
                for (lane, wide), w_ref in zip(chunks, w_refs):
                    w_ref[pl.ds(at, WROWS), :] = piece[
                        i * WROWS : (i + 1) * WROWS, lane : lane + wide
                    ]
                block += 1


def starts(lengths_ref, pos):
    start, end = jnp.zeros_like(pos), 0
    for r in range(REPOS):
        end = end + lengths_ref[0, r]
        start = start + jnp.where(pos >= end, lengths_ref[0, r], 0)
    return start


def norm_rows(src_ref, gain, out_ref, at, total):
    @pl.loop(0, total // 32)
    def _(i):
        value = src_ref[pl.ds(pl.multiple_of(i * 32, 32), 32), :].astype(jnp.float32)
        mean = jnp.mean(value * value, axis=1, keepdims=True)
        value = (value * lax.rsqrt(mean + norm_eps) * gain).astype(jnp.bfloat16)
        out_ref[pl.ds(pl.multiple_of(at + i * 32, 32), 32), :] = value


def prepare_kernel(info_ref, lengths_ref, hidden_ref, gain_ref, freq_ref, out_ref, cos_ref, sin_ref):
    norm_rows(hidden_ref, gain_ref[...], out_ref, 0, TOK)
    base = info_ref[3] * TOK - HALF + LENGTH
    sign = jnp.where(lax.broadcasted_iota(jnp.int32, (1, HEAD_DIM), 1) < HEAD_DIM // 2, -1.0, 1.0)

    @pl.loop(0, ROWS // 64)
    def _(i):
        at = pl.multiple_of(i * 64, 64)
        pos = (lax.broadcasted_iota(jnp.int32, (64, HEAD_DIM), 0) + (base + at)) & (LENGTH - 1)
        angle = (pos - starts(lengths_ref, pos)).astype(jnp.float32) * freq_ref[...]
        cos_ref[pl.ds(at, 64), :] = jnp.cos(angle)
        sin_ref[pl.ds(at, 64), :] = jnp.sin(angle) * sign


def prepare(info, lengths, hidden, gain, freq):
    table = jax.ShapeDtypeStruct((ROWS, HEAD_DIM), jnp.float32)
    return pl.pallas_call(
        prepare_kernel,
        out_shape=[jax.ShapeDtypeStruct((TOK, D), jnp.bfloat16), table, table],
        in_specs=[SM, SM, VM, VM, VM],
        out_specs=[VM] * 3,
        compiler_params=params(12),
        cost_estimate=pl.CostEstimate(
            flops=8 * TOK * D, bytes_accessed=4 * TOK * D, transcendentals=2 * ROWS * HEAD_DIM
        ),
        name="prepare",
    )(info, lengths, hidden, gain.reshape(1, D), freq)


def join_kernel(before_ref, own_ref, after_ref, gain_ref, out_ref):
    gain = gain_ref[...]
    norm_rows(before_ref, gain, out_ref, 0, HALF)
    norm_rows(after_ref, gain, out_ref, HALF + TOK, HALF)
    out_ref[HALF : HALF + TOK, :] = own_ref[...]


def join(before, own, after, gain):
    return pl.pallas_call(
        join_kernel,
        out_shape=jax.ShapeDtypeStruct((ROWS, D), jnp.bfloat16),
        in_specs=[VM] * 4,
        out_specs=VM,
        compiler_params=params(12),
        cost_estimate=pl.CostEstimate(
            flops=8 * TOK * D, bytes_accessed=4 * ROWS * D, transcendentals=TOK
        ),
        name="join",
    )(before, own, after, gain.reshape(1, D))


def rotate(value, cosine, sine):
    return value * cosine + pltpu.roll(value, HEAD_DIM // 2, 1) * sine


KV_CHUNKS = ((0, 256),)
Q_CHUNKS = ((0, 512), (512, 384))


def kv_kernel(count, info_ref, x_ref, bias_ref, cos_ref, sin_ref, *rest):
    out_ref, w_ref = rest[2 * count :]
    place_weights(info_ref, (rest[:count], rest[count : 2 * count]), KV_CHUNKS, (w_ref,))
    value = jnp.dot(x_ref[...], w_ref[...], preferred_element_type=jnp.float32)
    value = (value + bias_ref[...]).astype(jnp.bfloat16)
    keys = rotate(value[:, :128].astype(jnp.float32), cos_ref[...], sin_ref[...])
    out_ref[:, 0:128] = keys.astype(jnp.bfloat16)
    out_ref[:, 128:256] = value[:, 128:]


def q_kernel(count, info_ref, x_ref, bias_ref, cos_ref, sin_ref, *rest):
    out_ref, *w_refs = rest[2 * count :]
    place_weights(info_ref, (rest[:count], rest[count : 2 * count]), Q_CHUNKS, w_refs)
    for (at, wide), w_ref in zip(Q_CHUNKS, w_refs):
        value = jnp.dot(x_ref[...], w_ref[...], preferred_element_type=jnp.float32)
        value = (value + bias_ref[:, at : at + wide]).astype(jnp.bfloat16).astype(jnp.float32)
        for lane in range(0, wide, 128):
            head = rotate(value[:, lane : lane + 128], cos_ref[...], sin_ref[...])
            out_ref[:, at + lane : at + lane + 128] = head.astype(jnp.bfloat16)


def project(kernel, chunks, name, info, x, near, far, bias, cosine, sine):
    count, wide = len(near), sum(w for _, w in chunks)
    return pl.pallas_call(
        functools.partial(kernel, count),
        out_shape=jax.ShapeDtypeStruct((ROWS, wide), jnp.bfloat16),
        in_specs=[SM] + [VM] * (4 + 2 * count),
        out_specs=VM,
        scratch_shapes=[pltpu.VMEM((D, w), jnp.bfloat16) for _, w in chunks],
        compiler_params=params(20),
        cost_estimate=pl.CostEstimate(
            flops=2 * ROWS * D * wide, bytes_accessed=2 * (ROWS * D + D * wide), transcendentals=0
        ),
        name=name,
    )(info, x, bias, cosine, sine, *near, *far)


STACK = GROUP * HALF


def stacked(q_ref, tile):
    rows = slice(HALF * tile, HALF * (tile + 1))
    return jnp.concatenate(
        [q_ref[rows, h * HEAD_DIM : (h + 1) * HEAD_DIM] for h in range(GROUP)], 0
    )


def mask_of(info_ref, lengths_ref, tile, from_row, count):
    base = info_ref[3] * TOK - HALF + LENGTH
    key = lax.broadcasted_iota(jnp.int32, (HALF, count), 1) + (base - 1024 + from_row)
    key = key & (LENGTH - 1)
    pos = (lax.broadcasted_iota(jnp.int32, (HALF, 1), 0) + (base + HALF * tile)) & (LENGTH - 1)
    return jnp.where((key <= pos) & (key >= starts(lengths_ref, pos)), 0.0, MASKED)


def score(q_ref, tile, k, out_ref):
    out_ref[...] = lax.dot_general(
        stacked(q_ref, tile), k, (((1,), (1,)), ((), ())), preferred_element_type=jnp.float32
    )


def wide(column):
    return jnp.broadcast_to(column, (HALF, HEAD_DIM))


def first_kernel(info_ref, lengths_ref, q_ref, kv2_ref, kv0_ref, mix_ref, top_ref, sum_ref, kv_ref, *rest):
    score_refs, weight_refs = rest[:4], rest[4:]
    kv_ref[0:512, :] = kv2_ref[...]
    kv_ref[512:1024, :] = kv0_ref[...]
    counts = [640 + HALF * tile for tile in range(4)]
    score(q_ref, 0, kv_ref[0 : counts[0], 0:128], score_refs[0])
    for tile in range(4):
        if tile < 3:
            score(q_ref, tile + 1, kv_ref[0 : counts[tile + 1], 0:128], score_refs[tile + 1])
        mask = mask_of(info_ref, lengths_ref, tile, 512, counts[tile])
        for h in range(GROUP):
            part = slice(h * HALF, (h + 1) * HALF)
            at = slice(tile * STACK + h * HALF, tile * STACK + (h + 1) * HALF)
            value = score_refs[tile][part, :] * SCALE2 + mask
            top = jnp.max(value, axis=1, keepdims=True)
            weight = jnp.exp2(value - top)
            top_ref[at, :] = wide(top)
            sum_ref[at, :] = wide(jnp.sum(weight, axis=1, keepdims=True))
            weight_refs[tile][part, :] = weight.astype(jnp.bfloat16)
        mix_ref[tile * STACK : (tile + 1) * STACK, :] = jnp.dot(
            weight_refs[tile][...], kv_ref[0 : counts[tile], 128:256], preferred_element_type=jnp.float32
        )


def attention_first(info, lengths, q, kv2, kv0):
    state = jax.ShapeDtypeStruct((4 * STACK, HEAD_DIM), jnp.float32)
    counts = [640 + HALF * tile for tile in range(4)]
    return pl.pallas_call(
        first_kernel,
        out_shape=[state] * 3,
        in_specs=[SM, SM] + [VM] * 3,
        out_specs=[VM] * 3,
        scratch_shapes=[pltpu.VMEM((1024, 256), jnp.bfloat16)]
        + [pltpu.VMEM((STACK, n), jnp.float32) for n in counts]
        + [pltpu.VMEM((STACK, n), jnp.bfloat16) for n in counts],
        compiler_params=params(32),
        cost_estimate=pl.CostEstimate(
            flops=4 * STACK * sum(counts) * HEAD_DIM,
            bytes_accessed=8 << 20,
            transcendentals=STACK * sum(counts),
        ),
        name="attention_first",
    )(info, lengths, q, kv2, kv0)


def last_kernel(tiles, info_ref, lengths_ref, q_ref, kv_ref, mix_ref, top_ref, sum_ref, *rest):
    n = len(tiles)
    outs, score_refs, weight_refs, scale_refs = rest[:n], rest[n : 2 * n], rest[2 * n : 3 * n], rest[3 * n :]
    for tile, score_ref in zip(tiles, score_refs):
        score(q_ref, tile, kv_ref[HALF * tile : 512, 0:128], score_ref)
    for tile, out_ref, score_ref, weight_ref, scale_ref in zip(tiles, outs, score_refs, weight_refs, scale_refs):
        mask = mask_of(info_ref, lengths_ref, tile, HALF * tile, 512 - HALF * tile)
        for h in range(GROUP):
            part = slice(h * HALF, (h + 1) * HALF)
            at = slice(tile * STACK + h * HALF, tile * STACK + (h + 1) * HALF)
            value = score_ref[part, :] * SCALE2 + mask
            old = top_ref[at, 0:1]
            top = jnp.maximum(jnp.max(value, axis=1, keepdims=True), old)
            weight = jnp.exp2(value - top)
            keep = jnp.exp2(old - top)
            total = jnp.sum(weight, axis=1, keepdims=True) + keep * sum_ref[at, 0:1]
            scale_ref[part, 0:128] = wide(keep)
            scale_ref[part, 128:256] = wide(total)
            weight_ref[part, :] = weight.astype(jnp.bfloat16)
        mixed = jnp.dot(
            weight_ref[...], kv_ref[HALF * tile : 512, 128:256], preferred_element_type=jnp.float32
        )
        before = mix_ref[tile * STACK : (tile + 1) * STACK, :]
        mixed = (mixed + before * scale_ref[:, 0:128]) / scale_ref[:, 128:256]
        for h in range(GROUP):
            out_ref[:, h * HEAD_DIM : (h + 1) * HEAD_DIM] = mixed[h * HALF : (h + 1) * HALF].astype(
                jnp.bfloat16
            )


def attention_last(tiles, info, lengths, q, kv4, state):
    n = len(tiles)
    counts = [512 - HALF * tile for tile in tiles]
    return pl.pallas_call(
        functools.partial(last_kernel, tiles),
        out_shape=[jax.ShapeDtypeStruct((HALF, QC), jnp.bfloat16)] * n,
        in_specs=[SM, SM] + [VM] * 5,
        out_specs=[VM] * n,
        scratch_shapes=[pltpu.VMEM((STACK, c), jnp.float32) for c in counts]
        + [pltpu.VMEM((STACK, c), jnp.bfloat16) for c in counts]
        + [pltpu.VMEM((STACK, 256), jnp.float32) for _ in counts],
        compiler_params=params(20),
        cost_estimate=pl.CostEstimate(
            flops=4 * STACK * sum(counts) * HEAD_DIM,
            bytes_accessed=4 << 20,
            transcendentals=STACK * sum(counts),
        ),
        name="attention_last",
    )(info, lengths, q, kv4, *state)


def body(hidden, norm_gain, qkv_weight, qkv_bias, repo_lengths):
    z = lax.axis_index("ctx")
    odd = z % 2
    y, x, core = lax.axis_index("y"), lax.axis_index("x"), lax.axis_index("core")

    k_at, v_at = 1792 + odd * 128, 2048 + odd * 128
    kv_own = jnp.concatenate(
        [
            lax.dynamic_slice(qkv_weight, (0, k_at), (WROWS, 128)),
            lax.dynamic_slice(qkv_weight, (0, v_at), (WROWS, 128)),
        ],
        1,
    )
    kv_own, qkv_weight = lax.optimization_barrier((kv_own, qkv_weight))
    q_own = lax.dynamic_slice(qkv_weight, (0, odd * QC), (WROWS, QC))
    q_bias = lax.dynamic_slice(qkv_bias, (odd * QC,), (QC,)).reshape(1, QC)
    kv_bias = jnp.concatenate(
        [lax.dynamic_slice(qkv_bias, (k_at,), (128,)), lax.dynamic_slice(qkv_bias, (v_at,), (128,))]
    ).reshape(1, 256)

    info = jnp.stack([y, x, core, z]).astype(jnp.int32)
    freq = rope_base ** (-jnp.arange(0, HEAD_DIM, 2, dtype=jnp.float32) / HEAD_DIM)
    freq = jnp.concatenate([freq, freq]).reshape(1, HEAD_DIM)

    kv_row = first_phase(kv_own)
    before = ring(hidden[TOK - HALF :], "ctx", 1)
    after = ring(hidden[:HALF], "ctx", -1)
    q_row = first_phase(q_own)
    normed, cosine, sine = prepare(info, repo_lengths, hidden, norm_gain, freq)

    kv_row, normed, cosine, sine = lax.optimization_barrier((kv_row, normed, cosine, sine))
    kv_near = [kv_row, hop(kv_row, 1, 1), hop(kv_row, 1, -1), hop(kv_row, 1, 2)]
    q_below, q_above = hop(q_row, 1, 1), hop(q_row, 1, -1)
    kv_far = [ring(piece, "core", 1) for piece in kv_near]
    tokens = join(before, normed, after, norm_gain)
    kv0 = project(kv_kernel, KV_CHUNKS, "kv_project", info, tokens, kv_near, kv_far, kv_bias, cosine, sine)
    kv2 = ring(kv0, "ctx", 2)

    q_row, q_below, q_above, _ = lax.optimization_barrier((q_row, q_below, q_above, kv0))
    half = q_row.shape[0] // 2
    q_near = [q_row, q_below, q_above, hop(q_below[:half], 1, 1), hop(q_above[half:], 1, -1)]
    q_far = [ring(piece, "core", 1) for piece in q_near]
    kv4 = ring(kv2, "ctx", 2)
    q = project(q_kernel, Q_CHUNKS, "q_project", info, tokens, q_near, q_far, q_bias, cosine, sine)

    state = attention_first(info, repo_lengths, q, kv2, kv0)
    args = (info, repo_lengths, q, kv4, state)
    back, ahead = attention_last((0, 3), *args)
    low = ring(ahead, "ctx", 1)
    high = ring(back, "ctx", -1)
    own = jnp.concatenate(attention_last((1, 2), *args), 0)
    other = jnp.concatenate([low, high], 0)
    return jnp.where(
        odd == 0, jnp.concatenate([own, other], 1), jnp.concatenate([other, own], 1)
    )


def solution(mesh):
    fine = Mesh(mesh.devices.reshape(4, 4, 2, 8), ("y", "x", "core", "ctx"))
    grp = ("y", "x", "core")
    tokens = P(("y", "x", "core", "ctx"), None)
    in_specs = (tokens, P(), P(grp, None), P(), P(grp, None))
    return jax.shard_map(body, mesh=fine, in_specs=in_specs, out_specs=tokens, check_vma=False)
```

```python
import functools
import math

import jax
import jax.numpy as jnp
from jax import lax
from jax.experimental import pallas as pl
from jax.experimental.pallas import tpu as pltpu
from jax.sharding import Mesh
from jax.sharding import PartitionSpec as P

D = 3584
HEAD_DIM = 128
HEADS = 14
KV_HEADS = 2
GROUP = HEADS // KV_HEADS
LENGTH = 2048
TOK = 256
HALF = 128
ROWS = 512
WROWS = 112
REPOS = 6
QC = GROUP * HEAD_DIM
rope_base = 1000000.0
norm_eps = 1e-06
SCALE2 = HEAD_DIM ** (-0.5) * math.log2(math.e)
MASKED = -1e30
SIZES = {"x": 4, "y": 4, "core": 2, "ctx": 8}
ORDER = (0, -1, 1, 2)

SMALL = pl.CostEstimate(flops=1, bytes_accessed=1, transcendentals=0)
ANY = pl.BlockSpec(memory_space=pl.ANY)
HBM = pl.BlockSpec(memory_space=pltpu.HBM)
VM = pl.BlockSpec(memory_space=pltpu.VMEM)
SM = pl.BlockSpec(memory_space=pltpu.SMEM)


def params(mebibytes):
    return pltpu.CompilerParams(vmem_limit_bytes=mebibytes << 20)


def ring(value, axis, step):
    n = SIZES[axis]
    return lax.ppermute(value, axis, [(i, (i + step) % n) for i in range(n)])


def hop(value, phase, step):
    pairs = []
    for y in range(4):
        for x in range(4):
            for core in range(2):
                to_y, to_x = (y, (x + step) % 4) if core == phase else ((y + step) % 4, x)
                pairs.append(((y * 4 + x) * 2 + core, (to_y * 4 + to_x) * 2 + core))
    return lax.ppermute(value, ("y", "x", "core"), pairs)


def place_weights(info_ref, pieces, chunks, w_refs):
    y, x = info_ref[0], info_ref[1]
    for side in range(2):
        core = info_ref[2] if side == 0 else 1 - info_ref[2]
        block = 0
        for piece in pieces[side]:
            for i in range(piece.shape[0] // WROWS):
                outer, inner = ORDER[block // 4], ORDER[block % 4]
                dy = jnp.where(core == 0, outer, inner)
                dx = jnp.where(core == 0, inner, outer)
                chip = ((y + dy + 4) % 4) * 4 + (x + dx + 4) % 4
                at = pl.multiple_of((chip * 2 + core) * WROWS, 16)
                for (lane, wide), w_ref in zip(chunks, w_refs):
                    w_ref[pl.ds(at, WROWS), :] = piece[
                        i * WROWS : (i + 1) * WROWS, lane : lane + wide
                    ]
                block += 1


def starts(lengths_ref, pos):
    start, end = jnp.zeros_like(pos), 0
    for r in range(REPOS):
        end = end + lengths_ref[0, r]
        start = start + jnp.where(pos >= end, lengths_ref[0, r], 0)
    return start


def cut_kernel(info_ref, weight_ref, out_ref, sem):
    odd = info_ref[3] % 2
    copies = []
    for n, (src, dst, wide) in enumerate(
        ((1792 + odd * 128, 0, 128), (2048 + odd * 128, 128, 128), (odd * QC, 256, QC))
    ):
        copy = pltpu.make_async_copy(
            weight_ref.at[:, pl.ds(pl.multiple_of(src, 128), wide)],
            out_ref.at[:, pl.ds(dst, wide)],
            sem.at[n],
        )
        copy.start()
        copies.append(copy)
    for copy in copies:
        copy.wait()


def cut(info, weight):
    return pl.pallas_call(
        cut_kernel,
        out_shape=jax.ShapeDtypeStruct((WROWS, 256 + QC), jnp.bfloat16),
        in_specs=[SM, HBM],
        out_specs=VM,
        scratch_shapes=[pltpu.SemaphoreType.DMA((3,))],
        compiler_params=params(4),
        cost_estimate=SMALL,
        name="cut",
    )(info, weight)


def output_kernel(info_ref, own_top_ref, own_low_ref, other_top_ref, other_low_ref, out_ref, sem):
    odd = info_ref[3] % 2
    own_at = pl.multiple_of(odd * QC, 128)
    other_at = pl.multiple_of((1 - odd) * QC, 128)
    copies = []
    for n, (src_ref, row, at) in enumerate(
        (
            (own_top_ref, 0, own_at),
            (own_low_ref, HALF, own_at),
            (other_top_ref, 0, other_at),
            (other_low_ref, HALF, other_at),
        )
    ):
        copy = pltpu.make_async_copy(
            src_ref, out_ref.at[pl.ds(row, HALF), pl.ds(at, QC)], sem.at[n]
        )
        copy.start()
        copies.append(copy)
    for copy in copies:
        copy.wait()


def output(info, *parts):
    return pl.pallas_call(
        output_kernel,
        out_shape=jax.ShapeDtypeStruct((TOK, 2 * QC), jnp.bfloat16),
        in_specs=[SM] + [VM] * 4,
        out_specs=ANY,
        scratch_shapes=[pltpu.SemaphoreType.DMA((4,))],
        compiler_params=params(4),
        cost_estimate=SMALL,
        name="output",
    )(info, *parts)


def split_kernel(*refs):
    blocks, (kv_ref, q_ref) = refs[:4], refs[4:]
    for n, block_ref in enumerate(blocks):
        kv_ref[n * WROWS : (n + 1) * WROWS, :] = block_ref[:, 0:256]
        q_ref[n * WROWS : (n + 1) * WROWS, :] = block_ref[:, 256:]


def split(blocks):
    return pl.pallas_call(
        split_kernel,
        out_shape=[
            jax.ShapeDtypeStruct((4 * WROWS, 256), jnp.bfloat16),
            jax.ShapeDtypeStruct((4 * WROWS, QC), jnp.bfloat16),
        ],
        in_specs=[VM] * 4,
        out_specs=[VM] * 2,
        compiler_params=params(4),
        cost_estimate=SMALL,
        name="split",
    )(*blocks)


def norm_kernel(hidden_ref, gain_ref, low_ref, high_ref):
    gain = jnp.concatenate([gain_ref[n : n + 1, :] for n in range(D // 128)], 1)
    for half, out_ref in enumerate((low_ref, high_ref)):

        @pl.loop(0, HALF // 32)
        def _(i, half=half, out_ref=out_ref):
            at = pl.multiple_of(i * 32, 32)
            value = hidden_ref[pl.ds(half * HALF + at, 32), :].astype(jnp.float32)
            mean = jnp.mean(value * value, axis=1, keepdims=True)
            value = value * lax.rsqrt(mean + norm_eps) * gain
            out_ref[pl.ds(at, 32), :] = value.astype(jnp.bfloat16)


def norm(hidden, gain):
    return pl.pallas_call(
        norm_kernel,
        out_shape=[jax.ShapeDtypeStruct((HALF, D), jnp.bfloat16)] * 2,
        in_specs=[VM, VM],
        out_specs=[VM] * 2,
        compiler_params=params(12),
        cost_estimate=SMALL,
        name="norm",
    )(hidden, gain.reshape(D // 128, 128))


def tables_kernel(info_ref, lengths_ref, freq_ref, cos_ref, sin_ref):
    base = info_ref[3] * TOK - HALF + LENGTH
    sign = jnp.where(lax.broadcasted_iota(jnp.int32, (1, HEAD_DIM), 1) < HEAD_DIM // 2, -1.0, 1.0)

    @pl.loop(0, ROWS // 64)
    def _(i):
        at = pl.multiple_of(i * 64, 64)
        pos = (lax.broadcasted_iota(jnp.int32, (64, HEAD_DIM), 0) + (base + at)) & (LENGTH - 1)
        angle = (pos - starts(lengths_ref, pos)).astype(jnp.float32) * freq_ref[...]
        cos_ref[pl.ds(at, 64), :] = jnp.cos(angle)
        sin_ref[pl.ds(at, 64), :] = jnp.sin(angle) * sign


def tables(info, lengths, freq):
    return pl.pallas_call(
        tables_kernel,
        out_shape=[jax.ShapeDtypeStruct((ROWS, HEAD_DIM), jnp.float32)] * 2,
        in_specs=[SM, SM, VM],
        out_specs=[VM] * 2,
        compiler_params=params(4),
        cost_estimate=SMALL,
        name="tables",
    )(info, lengths, freq)


def rotate(value, cosine, sine):
    return value * cosine + pltpu.roll(value, HEAD_DIM // 2, 1) * sine


KV_CHUNKS = ((0, 256),)
Q_CHUNKS = ((0, 512), (512, 384))


def kv_kernel(count, info_ref, bias_ref, cos_ref, sin_ref, *rest):
    tokens, rest = rest[:4], rest[4:]
    out_ref, x_ref, w_ref = rest[2 * count :]
    place_weights(info_ref, (rest[:count], rest[count : 2 * count]), KV_CHUNKS, (w_ref,))
    for n, src_ref in enumerate(tokens):
        x_ref[n * HALF : (n + 1) * HALF, :] = src_ref[...]
    value = jnp.dot(x_ref[...], w_ref[...], preferred_element_type=jnp.float32)
    odd = info_ref[3] % 2
    k_at, v_at = (pl.multiple_of(at + odd * 128, 128) for at in (1792, 2048))
    bias = jnp.concatenate([bias_ref[:, pl.ds(k_at, 128)], bias_ref[:, pl.ds(v_at, 128)]], 1)
    value = (value + bias).astype(jnp.bfloat16)
    keys = rotate(value[:, :128].astype(jnp.float32), cos_ref[...], sin_ref[...])
    out_ref[:, 0:128] = keys.astype(jnp.bfloat16)
    out_ref[:, 128:256] = value[:, 128:]


def kv_project(info, tokens, near, far, bias, cosine, sine):
    count = len(near)
    return pl.pallas_call(
        functools.partial(kv_kernel, count),
        out_shape=[
            jax.ShapeDtypeStruct((ROWS, 256), jnp.bfloat16),
            jax.ShapeDtypeStruct((ROWS, D), jnp.bfloat16),
        ],
        in_specs=[SM] + [VM] * (7 + 2 * count),
        out_specs=[VM] * 2,
        scratch_shapes=[pltpu.VMEM((D, 256), jnp.bfloat16)],
        compiler_params=params(8),
        cost_estimate=SMALL,
        name="kv_project",
    )(info, bias, cosine, sine, *tokens, *near, *far)


def q_kernel(count, info_ref, x_ref, bias_ref, cos_ref, sin_ref, *rest):
    out_ref, *w_refs = rest[2 * count :]
    place_weights(info_ref, (rest[:count], rest[count : 2 * count]), Q_CHUNKS, w_refs)
    for (at, wide), w_ref in zip(Q_CHUNKS, w_refs):
        value = jnp.dot(x_ref[...], w_ref[...], preferred_element_type=jnp.float32)
        bias = bias_ref[:, pl.ds(pl.multiple_of((info_ref[3] % 2) * QC + at, 128), wide)]
        value = (value + bias).astype(jnp.bfloat16).astype(jnp.float32)
        for lane in range(0, wide, 128):
            head = rotate(value[:, lane : lane + 128], cos_ref[...], sin_ref[...])
            out_ref[:, at + lane : at + lane + 128] = head.astype(jnp.bfloat16)


def q_project(info, x, near, far, bias, cosine, sine):
    count = len(near)
    return pl.pallas_call(
        functools.partial(q_kernel, count),
        out_shape=jax.ShapeDtypeStruct((ROWS, QC), jnp.bfloat16),
        in_specs=[SM] + [VM] * (4 + 2 * count),
        out_specs=VM,
        scratch_shapes=[pltpu.VMEM((D, w), jnp.bfloat16) for _, w in Q_CHUNKS],
        compiler_params=params(14),
        cost_estimate=SMALL,
        name="q_project",
    )(info, x, bias, cosine, sine, *near, *far)


STACK = GROUP * HALF


def stacked(q_ref, tile):
    rows = slice(HALF * tile, HALF * (tile + 1))
    return jnp.concatenate(
        [q_ref[rows, h * HEAD_DIM : (h + 1) * HEAD_DIM] for h in range(GROUP)], 0
    )


def mask_of(info_ref, lengths_ref, tile, from_row, count):
    base = info_ref[3] * TOK - HALF + LENGTH
    key = lax.broadcasted_iota(jnp.int32, (HALF, count), 1) + (base - 1024 + from_row)
    key = key & (LENGTH - 1)
    pos = (lax.broadcasted_iota(jnp.int32, (HALF, 1), 0) + (base + HALF * tile)) & (LENGTH - 1)
    return jnp.where((key <= pos) & (key >= starts(lengths_ref, pos)), 0.0, MASKED)


def score(q_ref, tile, k, out_ref):
    out_ref[...] = lax.dot_general(
        stacked(q_ref, tile), k, (((1,), (1,)), ((), ())), preferred_element_type=jnp.float32
    )


def soften(score_ref, mask, part, top, weight_ref):
    for lane in range(0, mask.shape[1], 128):
        lanes = slice(lane, lane + 128)
        weight = jnp.exp2(score_ref[part, lanes] * SCALE2 + mask[:, lanes] - top)
        weight_ref[part, lanes] = weight.astype(jnp.bfloat16)


def top_of(score_ref, mask, part):
    best = score_ref[part, 0:128] * SCALE2 + mask[:, 0:128]
    for lane in range(128, mask.shape[1], 128):
        lanes = slice(lane, lane + 128)
        best = jnp.maximum(best, score_ref[part, lanes] * SCALE2 + mask[:, lanes])
    return jnp.broadcast_to(jnp.max(best, axis=1, keepdims=True), (HALF, HEAD_DIM))


def load_values(v_ref, *blocks):
    at = 0
    for block in blocks:
        v_ref[at : at + block.shape[0], 0:128] = block[:, 128:256]
        at += block.shape[0]
    v_ref[:, 128:256] = jnp.ones((at, 128), jnp.bfloat16)


def weigh(tiles, kept, from_row, q_ref, k_ref, v_ref, score_refs, weight_refs, info_ref, lengths_ref):
    def keys(n):
        first = max(from_row, HALF * tiles[n]) - from_row
        return slice(first, first + kept[n])

    score(q_ref, tiles[0], k_ref[keys(0), :], score_refs[0])
    for n, tile in enumerate(tiles):
        if n + 1 < len(tiles):
            score(q_ref, tiles[n + 1], k_ref[keys(n + 1), :], score_refs[n + 1])
        mask = mask_of(info_ref, lengths_ref, tile, max(from_row, HALF * tile), kept[n])
        tops = []
        for h in range(GROUP):
            part = slice(h * HALF, (h + 1) * HALF)
            top = top_of(score_refs[n], mask, part)
            tops.append(top)
            soften(score_refs[n], mask, part, top, weight_refs[n])
        yield n, tops, jnp.dot(weight_refs[n][...], v_ref[keys(n), :], preferred_element_type=jnp.float32)


def first_kernel(tiles, info_ref, lengths_ref, q_ref, kv2_ref, kv0_ref, mix_ref, top_ref, k_ref, v_ref, *rest):
    kept, n = [640 + HALF * tile for tile in tiles], len(tiles)
    k_ref[0:512, :] = kv2_ref[:, 0:128]
    k_ref[512:1024, :] = kv0_ref[:, 0:128]
    load_values(v_ref, kv2_ref, kv0_ref)
    for n, tops, mixed in weigh(
        tiles, kept, 512, q_ref, k_ref, v_ref, rest[:n], rest[n:], info_ref, lengths_ref
    ):
        for h, top in enumerate(tops):
            top_ref[n * STACK + h * HALF : n * STACK + (h + 1) * HALF, :] = top
        mix_ref[n * STACK : (n + 1) * STACK, :] = mixed


def attention_first(tiles, info, lengths, q, kv2, kv0):
    n, kept = len(tiles), [640 + HALF * tile for tile in tiles]
    return pl.pallas_call(
        functools.partial(first_kernel, tiles),
        out_shape=[
            jax.ShapeDtypeStruct((n * STACK, 256), jnp.float32),
            jax.ShapeDtypeStruct((n * STACK, 128), jnp.float32),
        ],
        in_specs=[SM, SM] + [VM] * 3,
        out_specs=[VM] * 2,
        scratch_shapes=[pltpu.VMEM((1024, 128), jnp.bfloat16), pltpu.VMEM((1024, 256), jnp.bfloat16)]
        + [pltpu.VMEM((STACK, c), jnp.float32) for c in kept]
        + [pltpu.VMEM((STACK, c), jnp.bfloat16) for c in kept],
        compiler_params=params(18),
        cost_estimate=SMALL,
        name="attention_first",
    )(info, lengths, q, kv2, kv0)


def full_kernel(tiles, info_ref, lengths_ref, q_ref, kv4_ref, kv2_ref, kv0_ref, *rest):
    n = len(tiles)
    outs, k_ref, v_ref, rest = rest[:n], rest[n], rest[n + 1], rest[n + 2 :]
    for at, block in enumerate((kv4_ref, kv2_ref, kv0_ref)):
        k_ref[at * 512 : (at + 1) * 512, :] = block[:, 0:128]
    load_values(v_ref, kv4_ref, kv2_ref, kv0_ref)
    for n, _, mixed in weigh(
        tiles, [1152] * n, 0, q_ref, k_ref, v_ref, rest[:n], rest[n:], info_ref, lengths_ref
    ):
        value = (mixed[:, 0:128] / mixed[:, 128:256]).astype(jnp.bfloat16)
        for h in range(GROUP):
            outs[n][:, h * HEAD_DIM : (h + 1) * HEAD_DIM] = value[h * HALF : (h + 1) * HALF]


def attention_full(tiles, info, lengths, q, kv4, kv2, kv0):
    n = len(tiles)
    return pl.pallas_call(
        functools.partial(full_kernel, tiles),
        out_shape=[jax.ShapeDtypeStruct((HALF, QC), jnp.bfloat16)] * n,
        in_specs=[SM, SM] + [VM] * 4,
        out_specs=[VM] * n,
        scratch_shapes=[pltpu.VMEM((1536, 128), jnp.bfloat16), pltpu.VMEM((1536, 256), jnp.bfloat16)]
        + [pltpu.VMEM((STACK, 1152), jnp.float32)] * n
        + [pltpu.VMEM((STACK, 1152), jnp.bfloat16)] * n,
        compiler_params=params(22),
        cost_estimate=SMALL,
        name="attention_full",
    )(info, lengths, q, kv4, kv2, kv0)


def last_kernel(tiles, info_ref, lengths_ref, q_ref, kv_ref, mix_ref, top_ref, *rest):
    n = len(tiles)
    outs, v_ref = rest[:n], rest[n]
    score_refs, weight_refs, keep_refs = rest[n + 1 : 2 * n + 1], rest[2 * n + 1 : 3 * n + 1], rest[3 * n + 1 :]
    load_values(v_ref, kv_ref)
    for tile, score_ref in zip(tiles, score_refs):
        score(q_ref, tile, kv_ref[HALF * tile : 512, 0:128], score_ref)
    for at, (tile, out_ref, score_ref, weight_ref, keep_ref) in enumerate(
        zip(tiles, outs, score_refs, weight_refs, keep_refs)
    ):
        mask = mask_of(info_ref, lengths_ref, tile, HALF * tile, 512 - HALF * tile)
        for h in range(GROUP):
            part = slice(h * HALF, (h + 1) * HALF)
            old = top_ref[at * STACK + h * HALF : at * STACK + (h + 1) * HALF, :]
            top = jnp.maximum(top_of(score_ref, mask, part), old)
            keep_ref[part, :] = jnp.exp2(old - top)
            soften(score_ref, mask, part, top, weight_ref)
        mixed = jnp.dot(
            weight_ref[...], v_ref[HALF * tile : 512, :], preferred_element_type=jnp.float32
        )
        for h in range(GROUP):
            part = slice(h * HALF, (h + 1) * HALF)
            before = mix_ref[at * STACK + h * HALF : at * STACK + (h + 1) * HALF, :]
            keep = keep_ref[part, :]
            total = mixed[part, 128:256] + before[:, 128:256] * keep
            value = (mixed[part, 0:128] + before[:, 0:128] * keep) / total
            out_ref[:, h * HEAD_DIM : (h + 1) * HEAD_DIM] = value.astype(jnp.bfloat16)


def attention_last(tiles, info, lengths, q, kv4, state):
    n = len(tiles)
    counts = [512 - HALF * tile for tile in tiles]
    return pl.pallas_call(
        functools.partial(last_kernel, tiles),
        out_shape=[jax.ShapeDtypeStruct((HALF, QC), jnp.bfloat16)] * n,
        in_specs=[SM, SM] + [VM] * 4,
        out_specs=[VM] * n,
        scratch_shapes=[pltpu.VMEM((512, 256), jnp.bfloat16)]
        + [pltpu.VMEM((STACK, c), jnp.float32) for c in counts]
        + [pltpu.VMEM((STACK, c), jnp.bfloat16) for c in counts]
        + [pltpu.VMEM((STACK, 128), jnp.float32) for _ in counts],
        compiler_params=params(12),
        cost_estimate=SMALL,
        name="attention_last",
    )(info, lengths, q, kv4, *state)


def body(hidden, norm_gain, qkv_weight, qkv_bias, repo_lengths):
    z = lax.axis_index("ctx")
    y, x, core = lax.axis_index("y"), lax.axis_index("x"), lax.axis_index("core")
    info = jnp.stack([y, x, core, z]).astype(jnp.int32)
    freq = rope_base ** (-jnp.arange(0, HEAD_DIM, 2, dtype=jnp.float32) / HEAD_DIM)
    freq = jnp.concatenate([freq, freq]).reshape(1, HEAD_DIM)
    bias = qkv_bias.reshape(1, -1)

    own = cut(info, qkv_weight)
    blocks = [own, hop(own, 0, 1), hop(own, 0, -1), hop(own, 0, 2)]
    low, high = norm(hidden, norm_gain)
    kv_row, q_row = split(blocks)
    before = ring(high, "ctx", 1)
    after = ring(low, "ctx", -1)

    kv_row, low, high = lax.optimization_barrier((kv_row, low, high))
    kv_near = [kv_row, hop(kv_row, 1, 1), hop(kv_row, 1, -1), hop(kv_row, 1, 2)]
    q_near = [q_row, hop(q_row, 1, 1), hop(q_row, 1, -1), hop(q_row, 1, 2)]
    cosine, sine = tables(info, repo_lengths, freq)
    *kv_near, cosine, sine = lax.optimization_barrier((*kv_near, cosine, sine))
    kv_near[3], before, after = lax.optimization_barrier((kv_near[3], before, after))
    kv_far = [ring(piece, "core", 1) for piece in kv_near]
    kv0, normed = kv_project(info, (before, low, high, after), kv_near, kv_far, bias, cosine, sine)
    kv2 = ring(kv0, "ctx", 2)

    *q_near, kv2 = lax.optimization_barrier((*q_near, kv2))
    kv4 = ring(kv2, "ctx", 2)
    q_far = [ring(piece, "core", 1) for piece in q_near]
    q = q_project(info, normed, q_near, q_far, bias, cosine, sine)

    state = attention_first((0, 3), info, repo_lengths, q, kv2, kv0)
    back, ahead = attention_last((0, 3), info, repo_lengths, q, kv4, state)
    other_top = ring(ahead, "ctx", 1)
    other_low = ring(back, "ctx", -1)
    own_top, own_low = attention_full((1, 2), info, repo_lengths, q, kv4, kv2, kv0)
    return output(info, own_top, own_low, other_top, other_low)


def solution(mesh):
    fine = Mesh(mesh.devices.reshape(4, 4, 2, 8), ("y", "x", "core", "ctx"))
    grp = ("y", "x", "core")
    tokens = P(("y", "x", "core", "ctx"), None)
    in_specs = (tokens, P(), P(grp, None), P(), P(grp, None))
    return jax.shard_map(body, mesh=fine, in_specs=in_specs, out_specs=tokens, check_vma=False)
```

```python
import functools
import math

import jax
import jax.numpy as jnp
from jax import lax
from jax.experimental import pallas as pl
from jax.experimental.pallas import tpu as pltpu
from jax.sharding import Mesh
from jax.sharding import PartitionSpec as P

D = 3584
HEAD_DIM = 128
HEADS = 14
KV_HEADS = 2
GROUP = HEADS // KV_HEADS
LENGTH = 2048
TOK = 256
HALF = 128
ROWS = 512
WROWS = 112
REPOS = 6
QC = GROUP * HEAD_DIM
rope_base = 1000000.0
norm_eps = 1e-06
SCALE2 = HEAD_DIM ** (-0.5) * math.log2(math.e)
MASKED = -1e30
SIZES = {"x": 4, "y": 4, "core": 2, "ctx": 8}
ORDER = (0, -1, 1, 2)

SMALL = pl.CostEstimate(flops=1, bytes_accessed=1, transcendentals=0)
ANY = pl.BlockSpec(memory_space=pl.ANY)
HBM = pl.BlockSpec(memory_space=pltpu.HBM)
VM = pl.BlockSpec(memory_space=pltpu.VMEM)
SM = pl.BlockSpec(memory_space=pltpu.SMEM)


def params(mebibytes):
    return pltpu.CompilerParams(vmem_limit_bytes=mebibytes << 20)


def ring(value, axis, step):
    n = SIZES[axis]
    return lax.ppermute(value, axis, [(i, (i + step) % n) for i in range(n)])


def hop(value, phase, step):
    pairs = []
    for y in range(4):
        for x in range(4):
            for core in range(2):
                to_y, to_x = (y, (x + step) % 4) if core == phase else ((y + step) % 4, x)
                pairs.append(((y * 4 + x) * 2 + core, (to_y * 4 + to_x) * 2 + core))
    return lax.ppermute(value, ("y", "x", "core"), pairs)


def place_weights(info_ref, pieces, chunks, w_refs):
    y, x = info_ref[0], info_ref[1]
    for side in range(2):
        core = info_ref[2] if side == 0 else 1 - info_ref[2]
        block = 0
        for piece in pieces[side]:
            for i in range(piece.shape[0] // WROWS):
                outer, inner = ORDER[block // 4], ORDER[block % 4]
                dy = jnp.where(core == 0, outer, inner)
                dx = jnp.where(core == 0, inner, outer)
                chip = ((y + dy + 4) % 4) * 4 + (x + dx + 4) % 4
                at = pl.multiple_of((chip * 2 + core) * WROWS, 16)
                for (lane, wide), w_ref in zip(chunks, w_refs):
                    w_ref[pl.ds(at, WROWS), :] = piece[
                        i * WROWS : (i + 1) * WROWS, lane : lane + wide
                    ]
                block += 1


def starts(lengths_ref, pos):
    start, end = jnp.zeros_like(pos), 0
    for r in range(REPOS):
        end = end + lengths_ref[0, r]
        start = start + jnp.where(pos >= end, lengths_ref[0, r], 0)
    return start


def cut_kernel(info_ref, weight_ref, out_ref, sem):
    odd = info_ref[3] % 2
    copies = []
    for n, (src, dst, wide) in enumerate(
        ((1792 + odd * 128, 0, 128), (2048 + odd * 128, 128, 128), (odd * QC, 256, QC))
    ):
        copy = pltpu.make_async_copy(
            weight_ref.at[:, pl.ds(pl.multiple_of(src, 128), wide)],
            out_ref.at[:, pl.ds(dst, wide)],
            sem.at[n],
        )
        copy.start()
        copies.append(copy)
    for copy in copies:
        copy.wait()


def cut(info, weight):
    return pl.pallas_call(
        cut_kernel,
        out_shape=jax.ShapeDtypeStruct((WROWS, 256 + QC), jnp.bfloat16),
        in_specs=[SM, HBM],
        out_specs=VM,
        scratch_shapes=[pltpu.SemaphoreType.DMA((3,))],
        compiler_params=params(4),
        cost_estimate=SMALL,
        name="cut",
    )(info, weight)


def output_kernel(info_ref, own_top_ref, own_low_ref, other_top_ref, other_low_ref, out_ref, sem):
    odd = info_ref[3] % 2
    own_at = pl.multiple_of(odd * QC, 128)
    other_at = pl.multiple_of((1 - odd) * QC, 128)
    copies = []
    for n, (src_ref, row, at) in enumerate(
        (
            (own_top_ref, 0, own_at),
            (own_low_ref, HALF, own_at),
            (other_top_ref, 0, other_at),
            (other_low_ref, HALF, other_at),
        )
    ):
        copy = pltpu.make_async_copy(
            src_ref, out_ref.at[pl.ds(row, HALF), pl.ds(at, QC)], sem.at[n]
        )
        copy.start()
        copies.append(copy)
    for copy in copies:
        copy.wait()


def output(info, *parts):
    return pl.pallas_call(
        output_kernel,
        out_shape=jax.ShapeDtypeStruct((TOK, 2 * QC), jnp.bfloat16),
        in_specs=[SM] + [VM] * 4,
        out_specs=ANY,
        scratch_shapes=[pltpu.SemaphoreType.DMA((4,))],
        compiler_params=params(4),
        cost_estimate=SMALL,
        name="output",
    )(info, *parts)


def split_kernel(*refs):
    blocks, (kv_ref, q_ref) = refs[:4], refs[4:]
    for n, block_ref in enumerate(blocks):
        kv_ref[n * WROWS : (n + 1) * WROWS, :] = block_ref[:, 0:256]
        q_ref[n * WROWS : (n + 1) * WROWS, :] = block_ref[:, 256:]


def split(blocks):
    return pl.pallas_call(
        split_kernel,
        out_shape=[
            jax.ShapeDtypeStruct((4 * WROWS, 256), jnp.bfloat16),
            jax.ShapeDtypeStruct((4 * WROWS, QC), jnp.bfloat16),
        ],
        in_specs=[VM] * 4,
        out_specs=[VM] * 2,
        compiler_params=params(4),
        cost_estimate=SMALL,
        name="split",
    )(*blocks)


def norm_kernel(hidden_ref, gain_ref, low_ref, high_ref):
    gain = jnp.concatenate([gain_ref[n : n + 1, :] for n in range(D // 128)], 1)
    for half, out_ref in enumerate((low_ref, high_ref)):

        @pl.loop(0, HALF // 32)
        def _(i, half=half, out_ref=out_ref):
            at = pl.multiple_of(i * 32, 32)
            value = hidden_ref[pl.ds(half * HALF + at, 32), :].astype(jnp.float32)
            mean = jnp.mean(value * value, axis=1, keepdims=True)
            value = value * lax.rsqrt(mean + norm_eps) * gain
            out_ref[pl.ds(at, 32), :] = value.astype(jnp.bfloat16)


def norm(hidden, gain):
    return pl.pallas_call(
        norm_kernel,
        out_shape=[jax.ShapeDtypeStruct((HALF, D), jnp.bfloat16)] * 2,
        in_specs=[VM, VM],
        out_specs=[VM] * 2,
        compiler_params=params(12),
        cost_estimate=SMALL,
        name="norm",
    )(hidden, gain.reshape(D // 128, 128))


def tables_kernel(info_ref, lengths_ref, freq_ref, cos_ref, sin_ref):
    base = info_ref[3] * TOK - HALF + LENGTH
    sign = jnp.where(lax.broadcasted_iota(jnp.int32, (1, HEAD_DIM), 1) < HEAD_DIM // 2, -1.0, 1.0)

    @pl.loop(0, ROWS // 64)
    def _(i):
        at = pl.multiple_of(i * 64, 64)
        pos = (lax.broadcasted_iota(jnp.int32, (64, HEAD_DIM), 0) + (base + at)) & (LENGTH - 1)
        angle = (pos - starts(lengths_ref, pos)).astype(jnp.float32) * freq_ref[...]
        cos_ref[pl.ds(at, 64), :] = jnp.cos(angle)
        sin_ref[pl.ds(at, 64), :] = jnp.sin(angle) * sign


def tables(info, lengths, freq):
    return pl.pallas_call(
        tables_kernel,
        out_shape=[jax.ShapeDtypeStruct((ROWS, HEAD_DIM), jnp.float32)] * 2,
        in_specs=[SM, SM, VM],
        out_specs=[VM] * 2,
        compiler_params=params(4),
        cost_estimate=SMALL,
        name="tables",
    )(info, lengths, freq)


def rotate(value, cosine, sine):
    return value * cosine + pltpu.roll(value, HEAD_DIM // 2, 1) * sine


KV_CHUNKS = ((0, 256),)
Q_CHUNKS = ((0, 512), (512, 384))


def kv_kernel(count, info_ref, bias_ref, cos_ref, sin_ref, *rest):
    tokens, rest = rest[:4], rest[4:]
    out_ref, x_ref, w_ref = rest[2 * count :]
    place_weights(info_ref, (rest[:count], rest[count : 2 * count]), KV_CHUNKS, (w_ref,))
    for n, src_ref in enumerate(tokens):
        x_ref[n * HALF : (n + 1) * HALF, :] = src_ref[...]
    value = jnp.dot(x_ref[...], w_ref[...], preferred_element_type=jnp.float32)
    odd = info_ref[3] % 2
    k_at, v_at = (pl.multiple_of(at + odd * 128, 128) for at in (1792, 2048))
    bias = jnp.concatenate([bias_ref[:, pl.ds(k_at, 128)], bias_ref[:, pl.ds(v_at, 128)]], 1)
    value = (value + bias).astype(jnp.bfloat16)
    keys = rotate(value[:, :128].astype(jnp.float32), cos_ref[...], sin_ref[...])
    out_ref[:, 0:128] = keys.astype(jnp.bfloat16)
    out_ref[:, 128:256] = value[:, 128:]


def kv_project(info, tokens, near, far, bias, cosine, sine):
    count = len(near)
    return pl.pallas_call(
        functools.partial(kv_kernel, count),
        out_shape=[
            jax.ShapeDtypeStruct((ROWS, 256), jnp.bfloat16),
            jax.ShapeDtypeStruct((ROWS, D), jnp.bfloat16),
        ],
        in_specs=[SM] + [VM] * (7 + 2 * count),
        out_specs=[VM] * 2,
        scratch_shapes=[pltpu.VMEM((D, 256), jnp.bfloat16)],
        compiler_params=params(8),
        cost_estimate=SMALL,
        name="kv_project",
    )(info, bias, cosine, sine, *tokens, *near, *far)


def q_kernel(count, info_ref, x_ref, bias_ref, cos_ref, sin_ref, *rest):
    out_ref, *w_refs = rest[2 * count :]
    place_weights(info_ref, (rest[:count], rest[count : 2 * count]), Q_CHUNKS, w_refs)
    for (at, wide), w_ref in zip(Q_CHUNKS, w_refs):
        value = jnp.dot(x_ref[...], w_ref[...], preferred_element_type=jnp.float32)
        bias = bias_ref[:, pl.ds(pl.multiple_of((info_ref[3] % 2) * QC + at, 128), wide)]
        value = (value + bias).astype(jnp.bfloat16).astype(jnp.float32)
        for lane in range(0, wide, 128):
            head = rotate(value[:, lane : lane + 128], cos_ref[...], sin_ref[...])
            out_ref[:, at + lane : at + lane + 128] = head.astype(jnp.bfloat16)


def q_project(info, x, near, far, bias, cosine, sine):
    count = len(near)
    return pl.pallas_call(
        functools.partial(q_kernel, count),
        out_shape=jax.ShapeDtypeStruct((ROWS, QC), jnp.bfloat16),
        in_specs=[SM] + [VM] * (4 + 2 * count),
        out_specs=VM,
        scratch_shapes=[pltpu.VMEM((D, w), jnp.bfloat16) for _, w in Q_CHUNKS],
        compiler_params=params(14),
        cost_estimate=SMALL,
        name="q_project",
    )(info, x, bias, cosine, sine, *near, *far)


STACK = GROUP * HALF


def stacked(q_ref, tile):
    rows = slice(HALF * tile, HALF * (tile + 1))
    return jnp.concatenate(
        [q_ref[rows, h * HEAD_DIM : (h + 1) * HEAD_DIM] for h in range(GROUP)], 0
    )


def mask_of(info_ref, lengths_ref, tile, from_row, count):
    base = info_ref[3] * TOK - HALF + LENGTH
    key = lax.broadcasted_iota(jnp.int32, (HALF, count), 1) + (base - 1024 + from_row)
    key = key & (LENGTH - 1)
    pos = (lax.broadcasted_iota(jnp.int32, (HALF, 1), 0) + (base + HALF * tile)) & (LENGTH - 1)
    return jnp.where((key <= pos) & (key >= starts(lengths_ref, pos)), 0.0, MASKED)


def score(q_ref, tile, k, out_ref):
    out_ref[...] = lax.dot_general(
        stacked(q_ref, tile), k, (((1,), (1,)), ((), ())), preferred_element_type=jnp.float32
    )


def soften(score_ref, mask, part, top, weight_ref):
    for lane in range(0, mask.shape[1], 128):
        lanes = slice(lane, lane + 128)
        weight = jnp.exp2(score_ref[part, lanes] * SCALE2 + mask[:, lanes] - top)
        weight_ref[part, lanes] = weight.astype(jnp.bfloat16)


def top_of(score_ref, mask, part):
    best = score_ref[part, 0:128] * SCALE2 + mask[:, 0:128]
    for lane in range(128, mask.shape[1], 128):
        lanes = slice(lane, lane + 128)
        best = jnp.maximum(best, score_ref[part, lanes] * SCALE2 + mask[:, lanes])
    return jnp.broadcast_to(jnp.max(best, axis=1, keepdims=True), (HALF, HEAD_DIM))


def load_values(v_ref, *blocks):
    at = 0
    for block in blocks:
        v_ref[at : at + block.shape[0], 0:128] = block[:, 128:256]
        at += block.shape[0]
    v_ref[:, 128:256] = jnp.ones((at, 128), jnp.bfloat16)


def weigh(tiles, kept, from_row, q_ref, k_ref, v_ref, score_refs, weight_refs, info_ref, lengths_ref):
    def keys(n):
        first = max(from_row, HALF * tiles[n]) - from_row
        return slice(first, first + kept[n])

    score(q_ref, tiles[0], k_ref[keys(0), :], score_refs[0])
    for n, tile in enumerate(tiles):
        if n + 1 < len(tiles):
            score(q_ref, tiles[n + 1], k_ref[keys(n + 1), :], score_refs[n + 1])
        mask = mask_of(info_ref, lengths_ref, tile, max(from_row, HALF * tile), kept[n])
        tops = []
        for h in range(GROUP):
            part = slice(h * HALF, (h + 1) * HALF)
            top = top_of(score_refs[n], mask, part)
            tops.append(top)
            soften(score_refs[n], mask, part, top, weight_refs[n])
        yield n, tops, jnp.dot(weight_refs[n][...], v_ref[keys(n), :], preferred_element_type=jnp.float32)


def first_kernel(tiles, info_ref, lengths_ref, q_ref, kv2_ref, kv0_ref, mix_ref, top_ref, k_ref, v_ref, *rest):
    kept, n = [640 + HALF * tile for tile in tiles], len(tiles)
    k_ref[0:512, :] = kv2_ref[:, 0:128]
    k_ref[512:1024, :] = kv0_ref[:, 0:128]
    load_values(v_ref, kv2_ref, kv0_ref)
    for n, tops, mixed in weigh(
        tiles, kept, 512, q_ref, k_ref, v_ref, rest[:n], rest[n:], info_ref, lengths_ref
    ):
        for h, top in enumerate(tops):
            top_ref[n * STACK + h * HALF : n * STACK + (h + 1) * HALF, :] = top
        mix_ref[n * STACK : (n + 1) * STACK, :] = mixed


def attention_first(tiles, info, lengths, q, kv2, kv0):
    n, kept = len(tiles), [640 + HALF * tile for tile in tiles]
    return pl.pallas_call(
        functools.partial(first_kernel, tiles),
        out_shape=[
            jax.ShapeDtypeStruct((n * STACK, 256), jnp.float32),
            jax.ShapeDtypeStruct((n * STACK, 128), jnp.float32),
        ],
        in_specs=[SM, SM] + [VM] * 3,
        out_specs=[VM] * 2,
        scratch_shapes=[pltpu.VMEM((1024, 128), jnp.bfloat16), pltpu.VMEM((1024, 256), jnp.bfloat16)]
        + [pltpu.VMEM((STACK, c), jnp.float32) for c in kept]
        + [pltpu.VMEM((STACK, c), jnp.bfloat16) for c in kept],
        compiler_params=params(18),
        cost_estimate=SMALL,
        name="attention_first",
    )(info, lengths, q, kv2, kv0)


def full_kernel(tiles, info_ref, lengths_ref, q_ref, kv4_ref, kv2_ref, kv0_ref, *rest):
    n = len(tiles)
    outs, k_ref, v_ref, rest = rest[:n], rest[n], rest[n + 1], rest[n + 2 :]
    for at, block in enumerate((kv4_ref, kv2_ref, kv0_ref)):
        k_ref[at * 512 : (at + 1) * 512, :] = block[:, 0:128]
    load_values(v_ref, kv4_ref, kv2_ref, kv0_ref)
    for n, _, mixed in weigh(
        tiles, [1152] * n, 0, q_ref, k_ref, v_ref, rest[:n], rest[n:], info_ref, lengths_ref
    ):
        value = (mixed[:, 0:128] / mixed[:, 128:256]).astype(jnp.bfloat16)
        for h in range(GROUP):
            outs[n][:, h * HEAD_DIM : (h + 1) * HEAD_DIM] = value[h * HALF : (h + 1) * HALF]


def attention_full(tiles, info, lengths, q, kv4, kv2, kv0):
    n = len(tiles)
    return pl.pallas_call(
        functools.partial(full_kernel, tiles),
        out_shape=[jax.ShapeDtypeStruct((HALF, QC), jnp.bfloat16)] * n,
        in_specs=[SM, SM] + [VM] * 4,
        out_specs=[VM] * n,
        scratch_shapes=[pltpu.VMEM((1536, 128), jnp.bfloat16), pltpu.VMEM((1536, 256), jnp.bfloat16)]
        + [pltpu.VMEM((STACK, 1152), jnp.float32)] * n
        + [pltpu.VMEM((STACK, 1152), jnp.bfloat16)] * n,
        compiler_params=params(22),
        cost_estimate=SMALL,
        name="attention_full",
    )(info, lengths, q, kv4, kv2, kv0)


def last_kernel(tiles, info_ref, lengths_ref, q_ref, kv_ref, mix_ref, top_ref, *rest):
    n = len(tiles)
    outs, v_ref = rest[:n], rest[n]
    score_refs, weight_refs, keep_refs = rest[n + 1 : 2 * n + 1], rest[2 * n + 1 : 3 * n + 1], rest[3 * n + 1 :]
    load_values(v_ref, kv_ref)
    for tile, score_ref in zip(tiles, score_refs):
        score(q_ref, tile, kv_ref[HALF * tile : 512, 0:128], score_ref)
    for at, (tile, out_ref, score_ref, weight_ref, keep_ref) in enumerate(
        zip(tiles, outs, score_refs, weight_refs, keep_refs)
    ):
        mask = mask_of(info_ref, lengths_ref, tile, HALF * tile, 512 - HALF * tile)
        for h in range(GROUP):
            part = slice(h * HALF, (h + 1) * HALF)
            old = top_ref[at * STACK + h * HALF : at * STACK + (h + 1) * HALF, :]
            top = jnp.maximum(top_of(score_ref, mask, part), old)
            keep_ref[part, :] = jnp.exp2(old - top)
            soften(score_ref, mask, part, top, weight_ref)
        mixed = jnp.dot(
            weight_ref[...], v_ref[HALF * tile : 512, :], preferred_element_type=jnp.float32
        )
        for h in range(GROUP):
            part = slice(h * HALF, (h + 1) * HALF)
            before = mix_ref[at * STACK + h * HALF : at * STACK + (h + 1) * HALF, :]
            keep = keep_ref[part, :]
            total = mixed[part, 128:256] + before[:, 128:256] * keep
            value = (mixed[part, 0:128] + before[:, 0:128] * keep) / total
            out_ref[:, h * HEAD_DIM : (h + 1) * HEAD_DIM] = value.astype(jnp.bfloat16)


def attention_last(tiles, info, lengths, q, kv4, state):
    n = len(tiles)
    counts = [512 - HALF * tile for tile in tiles]
    return pl.pallas_call(
        functools.partial(last_kernel, tiles),
        out_shape=[jax.ShapeDtypeStruct((HALF, QC), jnp.bfloat16)] * n,
        in_specs=[SM, SM] + [VM] * 4,
        out_specs=[VM] * n,
        scratch_shapes=[pltpu.VMEM((512, 256), jnp.bfloat16)]
        + [pltpu.VMEM((STACK, c), jnp.float32) for c in counts]
        + [pltpu.VMEM((STACK, c), jnp.bfloat16) for c in counts]
        + [pltpu.VMEM((STACK, 128), jnp.float32) for _ in counts],
        compiler_params=params(12),
        cost_estimate=SMALL,
        name="attention_last",
    )(info, lengths, q, kv4, *state)


def body(hidden, norm_gain, qkv_weight, qkv_bias, repo_lengths):
    z = lax.axis_index("ctx")
    y, x, core = lax.axis_index("y"), lax.axis_index("x"), lax.axis_index("core")
    info = jnp.stack([y, x, core, z]).astype(jnp.int32)
    freq = rope_base ** (-jnp.arange(0, HEAD_DIM, 2, dtype=jnp.float32) / HEAD_DIM)
    freq = jnp.concatenate([freq, freq]).reshape(1, HEAD_DIM)
    bias = qkv_bias.reshape(1, -1)

    own = cut(info, qkv_weight)
    blocks = [own, hop(own, 0, 1), hop(own, 0, -1), hop(own, 0, 2)]
    low, high = norm(hidden, norm_gain)
    cosine, sine = tables(info, repo_lengths, freq)
    blocks[3], cosine, sine = lax.optimization_barrier((blocks[3], cosine, sine))
    kv_row, q_row = split(blocks)
    before = ring(high, "ctx", 1)
    after = ring(low, "ctx", -1)

    kv_row, low, high = lax.optimization_barrier((kv_row, low, high))
    kv_near = [kv_row, hop(kv_row, 1, 1), hop(kv_row, 1, -1), hop(kv_row, 1, 2)]
    q_near = [q_row, hop(q_row, 1, 1), hop(q_row, 1, -1), hop(q_row, 1, 2)]
    kv_near[3], before, after = lax.optimization_barrier((kv_near[3], before, after))
    kv_far = [ring(piece, "core", 1) for piece in kv_near]
    kv0, normed = kv_project(info, (before, low, high, after), kv_near, kv_far, bias, cosine, sine)
    kv2 = ring(kv0, "ctx", 2)

    *q_near, kv2 = lax.optimization_barrier((*q_near, kv2))
    kv4 = ring(kv2, "ctx", 2)
    q_far = [ring(piece, "core", 1) for piece in q_near]
    q = q_project(info, normed, q_near, q_far, bias, cosine, sine)

    state = attention_first((0, 3), info, repo_lengths, q, kv2, kv0)
    back, ahead = attention_last((0, 3), info, repo_lengths, q, kv4, state)
    other_top = ring(ahead, "ctx", 1)
    other_low = ring(back, "ctx", -1)
    own_top, own_low = attention_full((1, 2), info, repo_lengths, q, kv4, kv2, kv0)
    return output(info, own_top, own_low, other_top, other_low)


def solution(mesh):
    fine = Mesh(mesh.devices.reshape(4, 4, 2, 8), ("y", "x", "core", "ctx"))
    grp = ("y", "x", "core")
    tokens = P(("y", "x", "core", "ctx"), None)
    in_specs = (tokens, P(), P(grp, None), P(), P(grp, None))
    return jax.shard_map(body, mesh=fine, in_specs=in_specs, out_specs=tokens, check_vma=False)
```

```python
import functools
import math

import jax
import jax.numpy as jnp
from jax import lax
from jax.experimental import pallas as pl
from jax.experimental.pallas import tpu as pltpu
from jax.sharding import Mesh
from jax.sharding import PartitionSpec as P

D = 3584
HEAD_DIM = 128
HEADS = 14
KV_HEADS = 2
GROUP = HEADS // KV_HEADS
LENGTH = 2048
TOK = 256
HALF = 128
ROWS = 512
WROWS = 112
REPOS = 6
QC = GROUP * HEAD_DIM
rope_base = 1000000.0
norm_eps = 1e-06
SCALE2 = HEAD_DIM ** (-0.5) * math.log2(math.e)
MASKED = -1e30
SIZES = {"x": 4, "y": 4, "core": 2, "ctx": 8}
ORDER = (0, -1, 1, 2)

SMALL = pl.CostEstimate(flops=1, bytes_accessed=1, transcendentals=0)
ANY = pl.BlockSpec(memory_space=pl.ANY)
HBM = pl.BlockSpec(memory_space=pltpu.HBM)
VM = pl.BlockSpec(memory_space=pltpu.VMEM)
SM = pl.BlockSpec(memory_space=pltpu.SMEM)


def params(mebibytes):
    return pltpu.CompilerParams(vmem_limit_bytes=mebibytes << 20)


def ring(value, axis, step):
    n = SIZES[axis]
    return lax.ppermute(value, axis, [(i, (i + step) % n) for i in range(n)])


def hop(value, phase, step):
    pairs = []
    for y in range(4):
        for x in range(4):
            for core in range(2):
                to_y, to_x = (y, (x + step) % 4) if core == phase else ((y + step) % 4, x)
                pairs.append(((y * 4 + x) * 2 + core, (to_y * 4 + to_x) * 2 + core))
    return lax.ppermute(value, ("y", "x", "core"), pairs)


def place_weights(info_ref, pieces, chunks, w_refs):
    y, x = info_ref[0], info_ref[1]
    for side in range(2):
        core = info_ref[2] if side == 0 else 1 - info_ref[2]
        block = 0
        for piece in pieces[side]:
            for i in range(piece.shape[0] // WROWS):
                outer, inner = ORDER[block // 4], ORDER[block % 4]
                dy = jnp.where(core == 0, outer, inner)
                dx = jnp.where(core == 0, inner, outer)
                chip = ((y + dy + 4) % 4) * 4 + (x + dx + 4) % 4
                at = pl.multiple_of((chip * 2 + core) * WROWS, 16)
                for (lane, wide), w_ref in zip(chunks, w_refs):
                    w_ref[pl.ds(at, WROWS), :] = piece[
                        i * WROWS : (i + 1) * WROWS, lane : lane + wide
                    ]
                block += 1


def starts(lengths_ref, pos):
    start, end = jnp.zeros_like(pos), 0
    for r in range(REPOS):
        end = end + lengths_ref[0, r]
        start = start + jnp.where(pos >= end, lengths_ref[0, r], 0)
    return start


def cut_kernel(info_ref, weight_ref, out_ref, sem):
    odd = info_ref[3] % 2
    copies = []
    for n, (src, dst, wide) in enumerate(
        ((1792 + odd * 128, 0, 128), (2048 + odd * 128, 128, 128), (odd * QC, 256, QC))
    ):
        copy = pltpu.make_async_copy(
            weight_ref.at[:, pl.ds(pl.multiple_of(src, 128), wide)],
            out_ref.at[:, pl.ds(dst, wide)],
            sem.at[n],
        )
        copy.start()
        copies.append(copy)
    for copy in copies:
        copy.wait()


def cut(info, weight):
    return pl.pallas_call(
        cut_kernel,
        out_shape=jax.ShapeDtypeStruct((WROWS, 256 + QC), jnp.bfloat16),
        in_specs=[SM, HBM],
        out_specs=VM,
        scratch_shapes=[pltpu.SemaphoreType.DMA((3,))],
        compiler_params=params(4),
        cost_estimate=SMALL,
        name="cut",
    )(info, weight)


def output_kernel(info_ref, own_top_ref, own_low_ref, other_top_ref, other_low_ref, out_ref, sem):
    odd = info_ref[3] % 2
    own_at = pl.multiple_of(odd * QC, 128)
    other_at = pl.multiple_of((1 - odd) * QC, 128)
    copies = []
    for n, (src_ref, row, at) in enumerate(
        (
            (own_top_ref, 0, own_at),
            (own_low_ref, HALF, own_at),
            (other_top_ref, 0, other_at),
            (other_low_ref, HALF, other_at),
        )
    ):
        copy = pltpu.make_async_copy(
            src_ref, out_ref.at[pl.ds(row, HALF), pl.ds(at, QC)], sem.at[n]
        )
        copy.start()
        copies.append(copy)
    for copy in copies:
        copy.wait()


def output(info, *parts):
    return pl.pallas_call(
        output_kernel,
        out_shape=jax.ShapeDtypeStruct((TOK, 2 * QC), jnp.bfloat16),
        in_specs=[SM] + [VM] * 4,
        out_specs=ANY,
        scratch_shapes=[pltpu.SemaphoreType.DMA((4,))],
        compiler_params=params(4),
        cost_estimate=SMALL,
        name="output",
    )(info, *parts)


def split_kernel(*refs):
    blocks, (kv_ref, q_ref) = refs[:4], refs[4:]
    for n, block_ref in enumerate(blocks):
        kv_ref[n * WROWS : (n + 1) * WROWS, :] = block_ref[:, 0:256]
        q_ref[n * WROWS : (n + 1) * WROWS, :] = block_ref[:, 256:]


def split(blocks):
    return pl.pallas_call(
        split_kernel,
        out_shape=[
            jax.ShapeDtypeStruct((4 * WROWS, 256), jnp.bfloat16),
            jax.ShapeDtypeStruct((4 * WROWS, QC), jnp.bfloat16),
        ],
        in_specs=[VM] * 4,
        out_specs=[VM] * 2,
        compiler_params=params(4),
        cost_estimate=SMALL,
        name="split",
    )(*blocks)


def norm_kernel(hidden_ref, gain_ref, low_ref, high_ref):
    gain = jnp.concatenate([gain_ref[n : n + 1, :] for n in range(D // 128)], 1)
    for half, out_ref in enumerate((low_ref, high_ref)):

        @pl.loop(0, HALF // 32)
        def _(i, half=half, out_ref=out_ref):
            at = pl.multiple_of(i * 32, 32)
            value = hidden_ref[pl.ds(half * HALF + at, 32), :].astype(jnp.float32)
            mean = jnp.mean(value * value, axis=1, keepdims=True)
            value = value * lax.rsqrt(mean + norm_eps) * gain
            out_ref[pl.ds(at, 32), :] = value.astype(jnp.bfloat16)


def norm(hidden, gain):
    return pl.pallas_call(
        norm_kernel,
        out_shape=[jax.ShapeDtypeStruct((HALF, D), jnp.bfloat16)] * 2,
        in_specs=[VM, VM],
        out_specs=[VM] * 2,
        compiler_params=params(12),
        cost_estimate=SMALL,
        name="norm",
    )(hidden, gain.reshape(D // 128, 128))


def tables_kernel(info_ref, lengths_ref, freq_ref, cos_ref, sin_ref):
    base = info_ref[3] * TOK - HALF + LENGTH
    sign = jnp.where(lax.broadcasted_iota(jnp.int32, (1, HEAD_DIM), 1) < HEAD_DIM // 2, -1.0, 1.0)

    @pl.loop(0, ROWS // 64)
    def _(i):
        at = pl.multiple_of(i * 64, 64)
        pos = (lax.broadcasted_iota(jnp.int32, (64, HEAD_DIM), 0) + (base + at)) & (LENGTH - 1)
        angle = (pos - starts(lengths_ref, pos)).astype(jnp.float32) * freq_ref[...]
        cos_ref[pl.ds(at, 64), :] = jnp.cos(angle)
        sin_ref[pl.ds(at, 64), :] = jnp.sin(angle) * sign


def tables(info, lengths, freq):
    return pl.pallas_call(
        tables_kernel,
        out_shape=[jax.ShapeDtypeStruct((ROWS, HEAD_DIM), jnp.float32)] * 2,
        in_specs=[SM, SM, VM],
        out_specs=[VM] * 2,
        compiler_params=params(4),
        cost_estimate=SMALL,
        name="tables",
    )(info, lengths, freq)


def rotate(value, cosine, sine):
    return value * cosine + pltpu.roll(value, HEAD_DIM // 2, 1) * sine


KV_CHUNKS = ((0, 256),)
Q_CHUNKS = ((0, 512), (512, 384))


def kv_kernel(count, info_ref, bias_ref, cos_ref, sin_ref, *rest):
    tokens, rest = rest[:4], rest[4:]
    out_ref, x_ref, w_ref = rest[2 * count :]
    place_weights(info_ref, (rest[:count], rest[count : 2 * count]), KV_CHUNKS, (w_ref,))
    for n, src_ref in enumerate(tokens):
        x_ref[n * HALF : (n + 1) * HALF, :] = src_ref[...]
    value = jnp.dot(x_ref[...], w_ref[...], preferred_element_type=jnp.float32)
    odd = info_ref[3] % 2
    k_at, v_at = (pl.multiple_of(at + odd * 128, 128) for at in (1792, 2048))
    bias = jnp.concatenate([bias_ref[:, pl.ds(k_at, 128)], bias_ref[:, pl.ds(v_at, 128)]], 1)
    value = (value + bias).astype(jnp.bfloat16)
    keys = rotate(value[:, :128].astype(jnp.float32), cos_ref[...], sin_ref[...])
    out_ref[:, 0:128] = keys.astype(jnp.bfloat16)
    out_ref[:, 128:256] = value[:, 128:]


def kv_project(info, tokens, near, far, bias, cosine, sine):
    count = len(near)
    return pl.pallas_call(
        functools.partial(kv_kernel, count),
        out_shape=[
            jax.ShapeDtypeStruct((ROWS, 256), jnp.bfloat16),
            jax.ShapeDtypeStruct((ROWS, D), jnp.bfloat16),
        ],
        in_specs=[SM] + [VM] * (7 + 2 * count),
        out_specs=[VM] * 2,
        scratch_shapes=[pltpu.VMEM((D, 256), jnp.bfloat16)],
        compiler_params=params(8),
        cost_estimate=SMALL,
        name="kv_project",
    )(info, bias, cosine, sine, *tokens, *near, *far)


def q_kernel(count, info_ref, x_ref, bias_ref, cos_ref, sin_ref, *rest):
    out_ref, *w_refs = rest[2 * count :]
    place_weights(info_ref, (rest[:count], rest[count : 2 * count]), Q_CHUNKS, w_refs)
    for (at, wide), w_ref in zip(Q_CHUNKS, w_refs):
        value = jnp.dot(x_ref[...], w_ref[...], preferred_element_type=jnp.float32)
        bias = bias_ref[:, pl.ds(pl.multiple_of((info_ref[3] % 2) * QC + at, 128), wide)]
        value = (value + bias).astype(jnp.bfloat16).astype(jnp.float32)
        for lane in range(0, wide, 128):
            head = rotate(value[:, lane : lane + 128], cos_ref[...], sin_ref[...])
            out_ref[:, at + lane : at + lane + 128] = head.astype(jnp.bfloat16)


def q_project(info, x, near, far, bias, cosine, sine):
    count = len(near)
    return pl.pallas_call(
        functools.partial(q_kernel, count),
        out_shape=jax.ShapeDtypeStruct((ROWS, QC), jnp.bfloat16),
        in_specs=[SM] + [VM] * (4 + 2 * count),
        out_specs=VM,
        scratch_shapes=[pltpu.VMEM((D, w), jnp.bfloat16) for _, w in Q_CHUNKS],
        compiler_params=params(14),
        cost_estimate=SMALL,
        name="q_project",
    )(info, x, bias, cosine, sine, *near, *far)


STACK = GROUP * HALF


def stacked(q_ref, tile):
    rows = slice(HALF * tile, HALF * (tile + 1))
    return jnp.concatenate(
        [q_ref[rows, h * HEAD_DIM : (h + 1) * HEAD_DIM] for h in range(GROUP)], 0
    )


def mask_of(info_ref, lengths_ref, tile, from_row, count):
    base = info_ref[3] * TOK - HALF + LENGTH
    key = lax.broadcasted_iota(jnp.int32, (HALF, count), 1) + (base - 1024 + from_row)
    key = key & (LENGTH - 1)
    pos = (lax.broadcasted_iota(jnp.int32, (HALF, 1), 0) + (base + HALF * tile)) & (LENGTH - 1)
    return jnp.where((key <= pos) & (key >= starts(lengths_ref, pos)), 0.0, MASKED)


def masks_kernel(info_ref, lengths_ref, out_ref):
    for tile in range(4):
        mask = mask_of(info_ref, lengths_ref, tile, HALF * tile, 1152)
        out_ref[HALF * tile : HALF * (tile + 1), :] = mask


def make_masks(info, lengths):
    return pl.pallas_call(
        masks_kernel,
        out_shape=jax.ShapeDtypeStruct((ROWS, 1152), jnp.float32),
        in_specs=[SM, SM],
        out_specs=VM,
        compiler_params=params(6),
        cost_estimate=SMALL,
        name="masks",
    )(info, lengths)


def mask_view(mask_ref, tile, from_row, count):
    first = from_row - HALF * tile
    return mask_ref.at[HALF * tile : HALF * (tile + 1), first : first + count]


def score(q_ref, tile, k, out_ref):
    out_ref[...] = lax.dot_general(
        stacked(q_ref, tile), k, (((1,), (1,)), ((), ())), preferred_element_type=jnp.float32
    )


def top_of(score_ref, mask, part):
    best = None
    for lane in range(0, mask.shape[1], 128):
        lanes = slice(lane, lane + 128)
        value = score_ref[part, lanes] * SCALE2 + mask[:, lanes]
        score_ref[part, lanes] = value
        best = value if best is None else jnp.maximum(best, value)
    return jnp.broadcast_to(jnp.max(best, axis=1, keepdims=True), (HALF, HEAD_DIM))


def soften(score_ref, part, top, weight_ref):
    for lane in range(0, score_ref.shape[1], 128):
        lanes = slice(lane, lane + 128)
        weight_ref[part, lanes] = jnp.exp2(score_ref[part, lanes] - top).astype(jnp.bfloat16)


def load_values(v_ref, *blocks):
    at = 0
    for block in blocks:
        v_ref[at : at + block.shape[0], 0:128] = block[:, 128:256]
        at += block.shape[0]
    v_ref[:, 128:256] = jnp.ones((at, 128), jnp.bfloat16)


def weigh(tiles, kept, from_row, q_ref, k_ref, v_ref, score_refs, weight_refs, mask_ref):
    def keys(n):
        first = max(from_row, HALF * tiles[n]) - from_row
        return slice(first, first + kept[n])

    score(q_ref, tiles[0], k_ref[keys(0), :], score_refs[0])
    for n, tile in enumerate(tiles):
        if n + 1 < len(tiles):
            score(q_ref, tiles[n + 1], k_ref[keys(n + 1), :], score_refs[n + 1])
        mask = mask_view(mask_ref, tile, max(from_row, HALF * tile), kept[n])
        tops = []
        for h in range(GROUP):
            part = slice(h * HALF, (h + 1) * HALF)
            top = top_of(score_refs[n], mask, part)
            tops.append(top)
            soften(score_refs[n], part, top, weight_refs[n])
        yield n, tops, jnp.dot(weight_refs[n][...], v_ref[keys(n), :], preferred_element_type=jnp.float32)


def first_kernel(tiles, mask_ref, q_ref, kv2_ref, kv0_ref, mix_ref, top_ref, k_ref, v_ref, *rest):
    kept, n = [640 + HALF * tile for tile in tiles], len(tiles)
    k_ref[0:512, :] = kv2_ref[:, 0:128]
    k_ref[512:1024, :] = kv0_ref[:, 0:128]
    load_values(v_ref, kv2_ref, kv0_ref)
    for n, tops, mixed in weigh(
        tiles, kept, 512, q_ref, k_ref, v_ref, rest[:n], rest[n:], mask_ref
    ):
        for h, top in enumerate(tops):
            top_ref[n * STACK + h * HALF : n * STACK + (h + 1) * HALF, :] = top
        mix_ref[n * STACK : (n + 1) * STACK, :] = mixed


def attention_first(tiles, masks, q, kv2, kv0):
    n, kept = len(tiles), [640 + HALF * tile for tile in tiles]
    return pl.pallas_call(
        functools.partial(first_kernel, tiles),
        out_shape=[
            jax.ShapeDtypeStruct((n * STACK, 256), jnp.float32),
            jax.ShapeDtypeStruct((n * STACK, 128), jnp.float32),
        ],
        in_specs=[VM] * 4,
        out_specs=[VM] * 2,
        scratch_shapes=[pltpu.VMEM((1024, 128), jnp.bfloat16), pltpu.VMEM((1024, 256), jnp.bfloat16)]
        + [pltpu.VMEM((STACK, c), jnp.float32) for c in kept]
        + [pltpu.VMEM((STACK, c), jnp.bfloat16) for c in kept],
        compiler_params=params(18),
        cost_estimate=SMALL,
        name="attention_first",
    )(masks, q, kv2, kv0)


def full_kernel(tiles, mask_ref, q_ref, kv4_ref, kv2_ref, kv0_ref, *rest):
    n = len(tiles)
    outs, k_ref, v_ref, rest = rest[:n], rest[n], rest[n + 1], rest[n + 2 :]
    for at, block in enumerate((kv4_ref, kv2_ref, kv0_ref)):
        k_ref[at * 512 : (at + 1) * 512, :] = block[:, 0:128]
    load_values(v_ref, kv4_ref, kv2_ref, kv0_ref)
    for n, _, mixed in weigh(
        tiles, [1152] * n, 0, q_ref, k_ref, v_ref, rest[:n], rest[n:], mask_ref
    ):
        value = (mixed[:, 0:128] / mixed[:, 128:256]).astype(jnp.bfloat16)
        for h in range(GROUP):
            outs[n][:, h * HEAD_DIM : (h + 1) * HEAD_DIM] = value[h * HALF : (h + 1) * HALF]


def attention_full(tiles, masks, q, kv4, kv2, kv0):
    n = len(tiles)
    return pl.pallas_call(
        functools.partial(full_kernel, tiles),
        out_shape=[jax.ShapeDtypeStruct((HALF, QC), jnp.bfloat16)] * n,
        in_specs=[VM] * 5,
        out_specs=[VM] * n,
        scratch_shapes=[pltpu.VMEM((1536, 128), jnp.bfloat16), pltpu.VMEM((1536, 256), jnp.bfloat16)]
        + [pltpu.VMEM((STACK, 1152), jnp.float32)] * n
        + [pltpu.VMEM((STACK, 1152), jnp.bfloat16)] * n,
        compiler_params=params(22),
        cost_estimate=SMALL,
        name="attention_full",
    )(masks, q, kv4, kv2, kv0)


def last_kernel(tiles, mask_ref, q_ref, kv_ref, mix_ref, top_ref, *rest):
    n = len(tiles)
    outs, v_ref = rest[:n], rest[n]
    score_refs, weight_refs, keep_refs = rest[n + 1 : 2 * n + 1], rest[2 * n + 1 : 3 * n + 1], rest[3 * n + 1 :]
    load_values(v_ref, kv_ref)
    for tile, score_ref in zip(tiles, score_refs):
        score(q_ref, tile, kv_ref[HALF * tile : 512, 0:128], score_ref)
    for at, (tile, out_ref, score_ref, weight_ref, keep_ref) in enumerate(
        zip(tiles, outs, score_refs, weight_refs, keep_refs)
    ):
        mask = mask_view(mask_ref, tile, HALF * tile, 512 - HALF * tile)
        for h in range(GROUP):
            part = slice(h * HALF, (h + 1) * HALF)
            old = top_ref[at * STACK + h * HALF : at * STACK + (h + 1) * HALF, :]
            top = jnp.maximum(top_of(score_ref, mask, part), old)
            keep_ref[part, :] = jnp.exp2(old - top)
            soften(score_ref, part, top, weight_ref)
        mixed = jnp.dot(
            weight_ref[...], v_ref[HALF * tile : 512, :], preferred_element_type=jnp.float32
        )
        for h in range(GROUP):
            part = slice(h * HALF, (h + 1) * HALF)
            before = mix_ref[at * STACK + h * HALF : at * STACK + (h + 1) * HALF, :]
            keep = keep_ref[part, :]
            total = mixed[part, 128:256] + before[:, 128:256] * keep
            value = (mixed[part, 0:128] + before[:, 0:128] * keep) / total
            out_ref[:, h * HEAD_DIM : (h + 1) * HEAD_DIM] = value.astype(jnp.bfloat16)


def attention_last(tiles, masks, q, kv4, state):
    n = len(tiles)
    counts = [512 - HALF * tile for tile in tiles]
    return pl.pallas_call(
        functools.partial(last_kernel, tiles),
        out_shape=[jax.ShapeDtypeStruct((HALF, QC), jnp.bfloat16)] * n,
        in_specs=[VM] * 5,
        out_specs=[VM] * n,
        scratch_shapes=[pltpu.VMEM((512, 256), jnp.bfloat16)]
        + [pltpu.VMEM((STACK, c), jnp.float32) for c in counts]
        + [pltpu.VMEM((STACK, c), jnp.bfloat16) for c in counts]
        + [pltpu.VMEM((STACK, 128), jnp.float32) for _ in counts],
        compiler_params=params(12),
        cost_estimate=SMALL,
        name="attention_last",
    )(masks, q, kv4, *state)


def body(hidden, norm_gain, qkv_weight, qkv_bias, repo_lengths):
    z = lax.axis_index("ctx")
    y, x, core = lax.axis_index("y"), lax.axis_index("x"), lax.axis_index("core")
    info = jnp.stack([y, x, core, z]).astype(jnp.int32)
    freq = rope_base ** (-jnp.arange(0, HEAD_DIM, 2, dtype=jnp.float32) / HEAD_DIM)
    freq = jnp.concatenate([freq, freq]).reshape(1, HEAD_DIM)
    bias = qkv_bias.reshape(1, -1)

    own = cut(info, qkv_weight)
    blocks = [own, hop(own, 0, 1), hop(own, 0, -1), hop(own, 0, 2)]
    low, high = norm(hidden, norm_gain)
    cosine, sine = tables(info, repo_lengths, freq)
    blocks[3], cosine, sine = lax.optimization_barrier((blocks[3], cosine, sine))
    kv_row, q_row = split(blocks)
    before = ring(high, "ctx", 1)
    after = ring(low, "ctx", -1)

    kv_row, low, high = lax.optimization_barrier((kv_row, low, high))
    kv_near = [kv_row, hop(kv_row, 1, 1), hop(kv_row, 1, -1), hop(kv_row, 1, 2)]
    q_near = [q_row, hop(q_row, 1, 1), hop(q_row, 1, -1), hop(q_row, 1, 2)]
    kv_near[3], before, after = lax.optimization_barrier((kv_near[3], before, after))
    kv_far = [ring(piece, "core", 1) for piece in kv_near]
    kv0, normed = kv_project(info, (before, low, high, after), kv_near, kv_far, bias, cosine, sine)
    kv2 = ring(kv0, "ctx", 2)

    masks = make_masks(info, repo_lengths)
    *q_near, kv2, masks = lax.optimization_barrier((*q_near, kv2, masks))
    kv4 = ring(kv2, "ctx", 2)
    q_far = [ring(piece, "core", 1) for piece in q_near]
    q = q_project(info, normed, q_near, q_far, bias, cosine, sine)

    state = attention_first((0, 3), masks, q, kv2, kv0)
    back, ahead = attention_last((0, 3), masks, q, kv4, state)
    other_top = ring(ahead, "ctx", 1)
    other_low = ring(back, "ctx", -1)
    own_top, own_low = attention_full((1, 2), masks, q, kv4, kv2, kv0)
    return output(info, own_top, own_low, other_top, other_low)


def solution(mesh):
    fine = Mesh(mesh.devices.reshape(4, 4, 2, 8), ("y", "x", "core", "ctx"))
    grp = ("y", "x", "core")
    tokens = P(("y", "x", "core", "ctx"), None)
    in_specs = (tokens, P(), P(grp, None), P(), P(grp, None))
    return jax.shard_map(body, mesh=fine, in_specs=in_specs, out_specs=tokens, check_vma=False)
```
